512 devices in a mesh: sec: 16 (over y, x_hi, core), op: 32 (over z, x_lo).
Axes of the slice: x: 4 (x_hi: 2, x_lo: 2; x = x_hi * 2 + x_lo), y: 4, z: 16, core: 2. Of those that a mesh axis runs over, the one named last changes fastest.
Arguments:
- wavefunction: bfloat16 [32, 256, 256], P('sec'), may hold values from -6 to 6
- diagonal: bfloat16 [32, 256, 256], P('sec'), may hold values from 1 to 4
- preconditioner: bfloat16 [32, 256, 256], P('sec'), may hold values from 0.25 to 1
- left_operator_blocks: bfloat16 [8192, 256, 256], P(('sec', 'op')), may hold values from -0.1875 to 0.1875
- right_operator_blocks: bfloat16 [8192, 256, 256], P(('sec', 'op')), may hold values from -0.375 to 0.375
- slot_source_sector: int32 [8192], P(('sec', 'op')), may hold values from 0 to 31
- slot_target_sector: int32 [8192], P(('sec', 'op')), may hold values from 0 to 1
- pair_count: int32 [512], P(('sec', 'op')), may hold values from 1 to 16, as said below
- left_dims: int32 [32], replicated, may hold values from 128 to 256, as said below
- right_dims: int32 [32], replicated, may hold values from 128 to 256, as said below
Outputs:
- correction: bfloat16 [32, 256, 256], P('sec')
- product_rows: float32 [32, 256, 256], P('sec', 'op')
- projected: float32 [3], replicated
The draws below stay inside these ranges and needn't reach their ends.
Inputs may be any that keep to these rules, and one draw needn't show every extreme that they name: `pair_count`: slots below a device's count hold pairs, the rest are ignored; some device has all 16 slots live. `left_dims`: some sector uses all 256 rows. `right_dims`: some sector uses all 256 columns.
All inputs are finite; a program needn't handle non-finite values.
Results may differ from the reference program's by a relative error of at most 0.003.
Values may be sent and summed in bfloat16 or wider, within the bound.
No kernel may reach another device: no remote copies, remote signals or barrier semaphores. Data moves between devices by JAX's collectives and lax.ppermute only.
A program may use at most 64 MiB of HBM per device.

```python
import math
import jax
import jax.numpy as jnp
from jax import lax

BLOCK_EXTENT = 256
DEVICE_SECTORS = 2
DEVICE_SLOTS = 16
SECTORS_TOTAL = 32
PAIR_SLOTS_TOTAL = 8192
N_SEC = 16
N_OP = 32


def draw_pair_count(key, part):
    first_key, second_key, third_key = jax.random.split(jax.random.fold_in(key, 11), 3)
    device_count = N_SEC * N_OP
    smaller = jnp.minimum(jax.random.randint(first_key, (device_count,), 1, DEVICE_SLOTS + 1), jax.random.randint(second_key, (device_count,), 1, DEVICE_SLOTS + 1))
    chosen = jax.random.randint(third_key, (), 0, device_count)
    return jnp.where(jnp.arange(device_count) == chosen, DEVICE_SLOTS, smaller).astype(jnp.int32)


def draw_dims(key, salt_value):
    first_key, second_key = jax.random.split(jax.random.fold_in(key, salt_value))
    sizes_drawn = jax.random.randint(first_key, (SECTORS_TOTAL,), BLOCK_EXTENT // 2, BLOCK_EXTENT + 1)
    chosen = jax.random.randint(second_key, (), 0, SECTORS_TOTAL)
    return jnp.where(jnp.arange(SECTORS_TOTAL) == chosen, BLOCK_EXTENT, sizes_drawn).astype(jnp.int32)


def draw_left_dims(key, part):
    return draw_dims(key, 21)


def draw_right_dims(key, part):
    return draw_dims(key, 22)


def place_ends(values, rng, low, largest):
    longest = values.shape.index(max(values.shape))
    spots = []
    for shift in (0, 1):
        where = [jax.random.randint(jax.random.fold_in(rng, axis), (), 0, length) for axis, length in enumerate(values.shape)]
        where[longest] = (where[longest] + shift) % values.shape[longest]
        spots.append(tuple(where))
    return values.at[spots[0]].set(low).at[spots[1]].set(largest)


def with_spikes(array, stream_key, source, target, parts, factor):
    owner, partner = [(jnp.arange(array.shape[dim]) // (array.shape[dim] // parts)).reshape([-1 if axis == dim else 1 for axis in range(array.ndim)]) for dim in (source, target)]
    chosen = jax.random.permutation(stream_key, parts)[partner]
    strong = (owner == chosen) | (owner == (partner + parts // 2) % parts)
    return jnp.where(strong, factor * array, array)


def block_scale(own_key, shape, shards, smallest, largest):
    factor_of = 1.0
    for position, shards_of in shards:
        draws = jax.random.uniform(jax.random.fold_in(jax.random.fold_in(own_key, 6), position), (shards_of,), jnp.float32, smallest / len(shards), largest / len(shards))
        factor_of = factor_of * jnp.repeat(jnp.exp(draws), shape[position] // shards_of).reshape((-1,) + (1,) * (len(shape) - 1 - position))
    return factor_of


def scatter_about(stream_key, shape, deviation, reach, shards=(), kind=jnp.bfloat16):
    gain = block_scale(stream_key, shape, shards, -0.22, 0.18) if shards else 1.0
    values = jax.random.normal(stream_key, shape, jnp.float32) * deviation * gain
    return jnp.minimum(jnp.maximum(values, -reach), reach).astype(kind)


def noise_with(stream_key, extent, width, reach, cuts, heavy, kind=jnp.bfloat16):
    values = width * jax.random.normal(stream_key, extent, jnp.float32)
    if cuts:
        values = values * block_scale(stream_key, extent, cuts, -0.22, 0.18)
    return jnp.clip(with_spikes(values, jax.random.fold_in(stream_key, 3), *heavy), -reach, reach).astype(kind)


def setup_inputs(seed: int = 0) -> dict:
    key_of = jax.random.split(jax.random.key(seed), 11)
    return {
        "wavefunction": scatter_about(key_of[0], (SECTORS_TOTAL, BLOCK_EXTENT, BLOCK_EXTENT), 1.0, 6.0, ((0, 16),)),
        "diagonal": jnp.clip(jnp.exp(math.log(4.0) - 1.3862944 * jax.random.uniform(key_of[1], (SECTORS_TOTAL, BLOCK_EXTENT, BLOCK_EXTENT), jnp.float32) ** block_scale(key_of[1], (SECTORS_TOTAL, BLOCK_EXTENT, BLOCK_EXTENT), ((0, 16),), -0.2, 0.2)), 1.0, 4.0).astype(jnp.bfloat16),
        "preconditioner": jnp.clip(jnp.exp(math.log(1.0) - 1.3862944 * jax.random.uniform(key_of[2], (SECTORS_TOTAL, BLOCK_EXTENT, BLOCK_EXTENT), jnp.float32) ** block_scale(key_of[2], (SECTORS_TOTAL, BLOCK_EXTENT, BLOCK_EXTENT), ((0, 16),), -0.2, 0.2)), 0.25, 1.0).astype(jnp.bfloat16),
        "left_operator_blocks": noise_with(key_of[3], (PAIR_SLOTS_TOTAL, BLOCK_EXTENT, BLOCK_EXTENT), (BLOCK_EXTENT * DEVICE_SLOTS * N_OP // (4 * DEVICE_SECTORS)) ** -0.5, 0.1875, ((0, 512),), (0, 1, 256, 6.0)),
        "right_operator_blocks": scatter_about(key_of[4], (PAIR_SLOTS_TOTAL, BLOCK_EXTENT, BLOCK_EXTENT), BLOCK_EXTENT ** -0.5, 0.375, ((0, 512),)),
        "slot_source_sector": place_ends(jax.random.randint(key_of[5], (PAIR_SLOTS_TOTAL,), 0, SECTORS_TOTAL), jax.random.fold_in(key_of[5], 1), 0, SECTORS_TOTAL - 1).astype(jnp.int32),
        "slot_target_sector": place_ends(jax.random.randint(key_of[6], (PAIR_SLOTS_TOTAL,), 0, DEVICE_SECTORS), jax.random.fold_in(key_of[6], 1), 0, DEVICE_SECTORS - 1).astype(jnp.int32),
        "pair_count": draw_pair_count(jax.random.fold_in(key_of[10], 71), 0),
        "left_dims": draw_left_dims(jax.random.fold_in(key_of[10], 71), 0),
        "right_dims": draw_right_dims(jax.random.fold_in(key_of[10], 71), 0),
    }


def block_mask(left_dims, right_dims, block_size):
    positions = jnp.arange(block_size, dtype=jnp.int32)
    return (positions[None, :, None] < left_dims[:, None, None]) & (positions[None, None, :] < right_dims[:, None, None])

def pair_sum(sources, left_operator_blocks, right_operator_blocks, slot_source_sector, target_sector, live_slot):
    zero_sum = jnp.zeros(sources.shape, jnp.float32)

    def add_pair(running, slot_index):

        def compute(running_now):
            source_block = sources[slot_source_sector[slot_index]]
            middle = jnp.dot(left_operator_blocks[slot_index], source_block, preferred_element_type=jnp.float32)
            contribution = jnp.dot(middle, right_operator_blocks[slot_index].astype(jnp.float32), precision=lax.Precision.HIGHEST, preferred_element_type=jnp.float32)
            return running_now.at[target_sector[slot_index]].add(contribution)

        def keep_same(running_now):
            return running_now
        return (lax.cond(live_slot[slot_index], compute, keep_same, running), None)
    slot_ids = jnp.arange(left_operator_blocks.shape[0], dtype=jnp.int32)
    result, _ = lax.scan(add_pair, zero_sum, slot_ids)
    return result

def reference(wavefunction, diagonal, preconditioner, left_operator_blocks, right_operator_blocks, slot_source_sector, slot_target_sector, pair_count, left_dims, right_dims):
    sector_total = wavefunction.shape[0]
    block_size = wavefunction.shape[1]
    entries = float(sector_total * block_size * block_size)
    used_mask = block_mask(left_dims, right_dims, block_size)
    slot_ids = jnp.arange(left_operator_blocks.shape[0], dtype=jnp.int32)
    device_ids = slot_ids // DEVICE_SLOTS
    live_slot = slot_ids % DEVICE_SLOTS < pair_count[device_ids]
    target_sector = (device_ids // N_OP * DEVICE_SECTORS + slot_target_sector).astype(jnp.int32)
    vector = jnp.where(used_mask, wavefunction, jnp.zeros_like(wavefunction))
    vector_float = vector.astype(jnp.float32)
    diag_float = diagonal.astype(jnp.float32)
    sigma_first = jnp.where(used_mask, diag_float * vector_float + pair_sum(vector, left_operator_blocks, right_operator_blocks, slot_source_sector, target_sector, live_slot), 0.0)
    norm_vector = jnp.sum(vector_float * vector_float)
    correlation = jnp.sum(vector_float * sigma_first)
    rayleigh = correlation / norm_vector
    residual = sigma_first - rayleigh * vector_float
    scaled = preconditioner.astype(jnp.float32) * residual
    along_vector = jnp.sum(vector_float * scaled)
    orthogonal = scaled - along_vector / norm_vector * vector_float
    square_norm = jnp.sum(orthogonal * orthogonal)
    correction = (orthogonal * lax.rsqrt(square_norm / entries + 1e-06)).astype(jnp.bfloat16)
    corr_float = correction.astype(jnp.float32)
    product_rows = jnp.where(used_mask, diag_float * corr_float + pair_sum(correction, left_operator_blocks, right_operator_blocks, slot_source_sector, target_sector, live_slot), 0.0)
    cross_term = jnp.sum(vector_float * product_rows)
    self_term = jnp.sum(corr_float * product_rows)
    projected = jnp.stack([rayleigh, cross_term * lax.rsqrt(norm_vector * entries), self_term / entries])
    return (correction, product_rows, projected)
```

```python
import functools

import jax
import jax.numpy as jnp
from jax import lax
from jax.experimental import pallas as pl
from jax.experimental.pallas import tpu as pltpu
from jax.sharding import PartitionSpec as P


def block_mask(left_dims, right_dims, block_size):
    positions = jnp.arange(block_size, dtype=jnp.int32)
    return (positions[None, :, None] < left_dims[:, None, None]) & (
        positions[None, None, :] < right_dims[:, None, None]
    )


def gather_blocks(value, axis_name, count):
    parts = [value]
    for shift in range(1, count):
        parts.append(
            lax.ppermute(value, axis_name, [(i, (i - shift) % count) for i in range(count)])
        )
    return jnp.stack(parts, 0)


def ordered_gather(value, axis_name, count):
    stacked = gather_blocks(value, axis_name, count)
    index = lax.axis_index(axis_name)
    return jnp.roll(stacked, index, axis=0)


def reduce_vector(values, axis_name, count):
    return jnp.sum(ordered_gather(values, axis_name, count), axis=0)


def reduce_scatter_rows(partial_value, axis_name, count):
    rows = partial_value.shape[1] // count
    index = lax.axis_index(axis_name)
    total = lax.dynamic_slice_in_dim(partial_value, index * rows, rows, 1)
    for shift in range(1, count):
        chunk = lax.dynamic_slice_in_dim(
            partial_value, ((index + shift) % count) * rows, rows, 1
        )
        total = total + lax.ppermute(
            chunk, axis_name, [(i, (i + shift) % count) for i in range(count)]
        )
    return total


def pair_kernel(src_ref, tgt_ref, cnt_ref, s_ref, l_ref, r_ref, o_ref):
    k = pl.program_id(0)

    @pl.when(k == 0)
    def _():
        o_ref[...] = jnp.zeros_like(o_ref)

    @pl.when(k < cnt_ref[0])
    def _():
        middle = jnp.dot(l_ref[0], s_ref[0], preferred_element_type=jnp.float32)
        high = middle.astype(jnp.bfloat16)
        low = (middle - high.astype(jnp.float32)).astype(jnp.bfloat16)
        right = r_ref[0]
        contribution = jnp.dot(high, right, preferred_element_type=jnp.float32) + jnp.dot(
            low, right, preferred_element_type=jnp.float32
        )
        t = tgt_ref[k]
        o_ref[t] = o_ref[t] + contribution


def pair_partial(sources, left_blocks, right_blocks, source_index, target_index, live_count, sector_count):
    slots, block_size, _ = left_blocks.shape
    n_sources = sources.shape[0]

    def live_slot(k, cnt):
        return jnp.minimum(k, jnp.clip(cnt[0] - 1, 0, slots - 1))

    def source_map(k, src, tgt, cnt):
        return (jnp.clip(src[live_slot(k, cnt)], 0, n_sources - 1), 0, 0)

    def operator_map(k, src, tgt, cnt):
        return (live_slot(k, cnt), 0, 0)

    block = (1, block_size, block_size)
    grid_spec = pltpu.PrefetchScalarGridSpec(
        num_scalar_prefetch=3,
        grid=(slots,),
        in_specs=[
            pl.BlockSpec(block, source_map),
            pl.BlockSpec(block, operator_map),
            pl.BlockSpec(block, operator_map),
        ],
        out_specs=pl.BlockSpec(
            (sector_count, block_size, block_size), lambda k, src, tgt, cnt: (0, 0, 0)
        ),
    )
    return pl.pallas_call(
        pair_kernel,
        grid_spec=grid_spec,
        out_shape=jax.ShapeDtypeStruct((sector_count, block_size, block_size), jnp.float32),
        compiler_params=pltpu.CompilerParams(dimension_semantics=("arbitrary",)),
    )(source_index, target_index, live_count, sources, left_blocks, right_blocks)


def on_device(
    wavefunction,
    diagonal,
    preconditioner,
    left_operator_blocks,
    right_operator_blocks,
    slot_source_sector,
    slot_target_sector,
    pair_count,
    left_dims,
    right_dims,
):
    sector_count = wavefunction.shape[0]
    block_size = wavefunction.shape[1]
    n_sec = lax.axis_size("sec")
    n_op = lax.axis_size("op")
    share_rows = block_size // n_op
    sec_index = lax.axis_index("sec")
    op_index = lax.axis_index("op")
    first_sector = sec_index * sector_count
    row_start = op_index * share_rows
    entries = float(left_dims.shape[0] * block_size * block_size)
    own_mask = block_mask(
        lax.dynamic_slice_in_dim(left_dims, first_sector, sector_count),
        lax.dynamic_slice_in_dim(right_dims, first_sector, sector_count),
        block_size,
    )
    own_vector = jnp.where(own_mask, wavefunction, jnp.zeros_like(wavefunction))
    diag_view = diagonal.astype(jnp.float32)
    scale_view = preconditioner.astype(jnp.float32)
    vector_view = own_vector.astype(jnp.float32)

    owner = slot_source_sector // sector_count
    source_index = ((owner - sec_index) % n_sec) * sector_count + slot_source_sector % sector_count
    target_index = jnp.clip(slot_target_sector, 0, sector_count - 1)
    live_count = pair_count

    def apply_partial(field):
        sources = gather_blocks(field, "sec", n_sec).reshape(
            (n_sec * sector_count, block_size, block_size)
        )
        partial_value = pair_partial(
            sources,
            left_operator_blocks,
            right_operator_blocks,
            source_index,
            target_index,
            live_count,
            sector_count,
        )
        return reduce_scatter_rows(partial_value, "op", n_op)

    pair_rows = apply_partial(own_vector)
    pairs_first = (
        ordered_gather(pair_rows, "op", n_op)
        .transpose(1, 0, 2, 3)
        .reshape((sector_count, block_size, block_size))
    )
    sigma_first = jnp.where(own_mask, diag_view * vector_view + pairs_first, 0.0)
    norm_vector, correlation = reduce_vector(
        jnp.stack([jnp.sum(vector_view * vector_view), jnp.sum(vector_view * sigma_first)]),
        "sec",
        n_sec,
    )
    rayleigh = correlation / norm_vector
    residual = sigma_first - rayleigh * vector_view
    scaled = scale_view * residual
    along_vector, scaled_square = reduce_vector(
        jnp.stack([jnp.sum(vector_view * scaled), jnp.sum(scaled * scaled)]), "sec", n_sec
    )
    orthogonal = scaled - along_vector / norm_vector * vector_view
    square_norm = scaled_square - along_vector * along_vector / norm_vector
    corr_view = (orthogonal * lax.rsqrt(square_norm / entries + 1e-06)).astype(jnp.bfloat16)

    pairs_second = apply_partial(corr_view)
    mask_rows = lax.dynamic_slice_in_dim(own_mask, row_start, share_rows, 1)
    diag_rows = lax.dynamic_slice_in_dim(diag_view, row_start, share_rows, 1)
    corr_rows = lax.dynamic_slice_in_dim(corr_view, row_start, share_rows, 1).astype(jnp.float32)
    vector_rows = lax.dynamic_slice_in_dim(vector_view, row_start, share_rows, 1)
    product_rows = jnp.where(mask_rows, diag_rows * corr_rows + pairs_second, 0.0)
    local_terms = jnp.stack(
        [jnp.sum(vector_rows * product_rows), jnp.sum(corr_rows * product_rows)]
    )
    cross_term, self_term = reduce_vector(reduce_vector(local_terms, "op", n_op), "sec", n_sec)
    projected = jnp.stack(
        [rayleigh, cross_term * lax.rsqrt(norm_vector * entries), self_term / entries]
    )
    return (corr_view, product_rows, projected)


def solution(mesh):
    in_specs = (
        P("sec", None, None),
        P("sec", None, None),
        P("sec", None, None),
        P(("sec", "op"), None, None),
        P(("sec", "op"), None, None),
        P(("sec", "op")),
        P(("sec", "op")),
        P(("sec", "op")),
        P(),
        P(),
    )
    out_specs = (P("sec", None, None), P("sec", "op", None), P())
    return jax.shard_map(
        on_device, mesh=mesh, in_specs=in_specs, out_specs=out_specs, check_vma=False
    )
```

```python
import functools

import jax
import jax.numpy as jnp
from jax import lax
from jax.experimental import pallas as pl
from jax.experimental.pallas import tpu as pltpu
from jax.sharding import PartitionSpec as P


def block_mask(left_dims, right_dims, block_size):
    positions = jnp.arange(block_size, dtype=jnp.int32)
    return (positions[None, :, None] < left_dims[:, None, None]) & (
        positions[None, None, :] < right_dims[:, None, None]
    )


def gather_blocks(value, axis_name, count):
    parts = [value]
    for shift in range(1, count):
        parts.append(
            lax.ppermute(value, axis_name, [(i, (i - shift) % count) for i in range(count)])
        )
    return jnp.stack(parts, 0)


def ordered_gather(value, axis_name, count):
    spread = jnp.broadcast_to(value[None], (count,) + value.shape)
    return lax.all_to_all(spread, axis_name, 0, 0, tiled=True)


def reduce_vector(values, axis_name, count):
    return jnp.sum(ordered_gather(values, axis_name, count), axis=0)


def reduce_scatter_rows(partial_value, axis_name, count):
    sectors, rows, cols = partial_value.shape
    chunks = partial_value.reshape((sectors, count, rows // count, cols)).transpose(1, 0, 2, 3)
    received = lax.all_to_all(chunks, axis_name, 0, 0, tiled=True)
    return jnp.sum(received, axis=0)


def pair_kernel(src_ref, tgt_ref, cnt_ref, s_ref, l_ref, r_ref, o_ref):
    k = pl.program_id(0)

    @pl.when(k == 0)
    def _():
        o_ref[...] = jnp.zeros_like(o_ref)

    @pl.when(k < cnt_ref[0])
    def _():
        middle = jnp.dot(l_ref[0], s_ref[0], preferred_element_type=jnp.float32)
        high = middle.astype(jnp.bfloat16)
        low = (middle - high.astype(jnp.float32)).astype(jnp.bfloat16)
        right = r_ref[0]
        contribution = jnp.dot(high, right, preferred_element_type=jnp.float32) + jnp.dot(
            low, right, preferred_element_type=jnp.float32
        )
        t = tgt_ref[k]
        o_ref[t] = o_ref[t] + contribution


def pair_partial(sources, left_blocks, right_blocks, source_index, target_index, live_count, sector_count):
    slots, block_size, _ = left_blocks.shape
    n_sources = sources.shape[0]

    def live_slot(k, cnt):
        return jnp.minimum(k, jnp.clip(cnt[0] - 1, 0, slots - 1))

    def source_map(k, src, tgt, cnt):
        return (jnp.clip(src[live_slot(k, cnt)], 0, n_sources - 1), 0, 0)

    def operator_map(k, src, tgt, cnt):
        return (live_slot(k, cnt), 0, 0)

    block = (1, block_size, block_size)
    grid_spec = pltpu.PrefetchScalarGridSpec(
        num_scalar_prefetch=3,
        grid=(slots,),
        in_specs=[
            pl.BlockSpec(block, source_map),
            pl.BlockSpec(block, operator_map),
            pl.BlockSpec(block, operator_map),
        ],
        out_specs=pl.BlockSpec(
            (sector_count, block_size, block_size), lambda k, src, tgt, cnt: (0, 0, 0)
        ),
    )
    return pl.pallas_call(
        pair_kernel,
        grid_spec=grid_spec,
        out_shape=jax.ShapeDtypeStruct((sector_count, block_size, block_size), jnp.float32),
        compiler_params=pltpu.CompilerParams(dimension_semantics=("arbitrary",)),
    )(source_index, target_index, live_count, sources, left_blocks, right_blocks)


def on_device(
    wavefunction,
    diagonal,
    preconditioner,
    left_operator_blocks,
    right_operator_blocks,
    slot_source_sector,
    slot_target_sector,
    pair_count,
    left_dims,
    right_dims,
):
    sector_count = wavefunction.shape[0]
    block_size = wavefunction.shape[1]
    n_sec = lax.axis_size("sec")
    n_op = lax.axis_size("op")
    share_rows = block_size // n_op
    sec_index = lax.axis_index("sec")
    op_index = lax.axis_index("op")
    first_sector = sec_index * sector_count
    row_start = op_index * share_rows
    entries = float(left_dims.shape[0] * block_size * block_size)
    own_mask = block_mask(
        lax.dynamic_slice_in_dim(left_dims, first_sector, sector_count),
        lax.dynamic_slice_in_dim(right_dims, first_sector, sector_count),
        block_size,
    )
    own_vector = jnp.where(own_mask, wavefunction, jnp.zeros_like(wavefunction))
    diag_view = diagonal.astype(jnp.float32)
    scale_view = preconditioner.astype(jnp.float32)
    vector_view = own_vector.astype(jnp.float32)

    owner = slot_source_sector // sector_count
    source_index = ((owner - sec_index) % n_sec) * sector_count + slot_source_sector % sector_count
    target_index = jnp.clip(slot_target_sector, 0, sector_count - 1)
    live_count = pair_count

    def apply_partial(field):
        sources = gather_blocks(field, "sec", n_sec).reshape(
            (n_sec * sector_count, block_size, block_size)
        )
        partial_value = pair_partial(
            sources,
            left_operator_blocks,
            right_operator_blocks,
            source_index,
            target_index,
            live_count,
            sector_count,
        )
        return reduce_scatter_rows(partial_value, "op", n_op)

    pair_rows = apply_partial(own_vector)
    pairs_first = (
        ordered_gather(pair_rows, "op", n_op)
        .transpose(1, 0, 2, 3)
        .reshape((sector_count, block_size, block_size))
    )
    sigma_first = jnp.where(own_mask, diag_view * vector_view + pairs_first, 0.0)
    norm_vector, correlation = reduce_vector(
        jnp.stack([jnp.sum(vector_view * vector_view), jnp.sum(vector_view * sigma_first)]),
        "sec",
        n_sec,
    )
    rayleigh = correlation / norm_vector
    residual = sigma_first - rayleigh * vector_view
    scaled = scale_view * residual
    along_vector, scaled_square = reduce_vector(
        jnp.stack([jnp.sum(vector_view * scaled), jnp.sum(scaled * scaled)]), "sec", n_sec
    )
    orthogonal = scaled - along_vector / norm_vector * vector_view
    square_norm = scaled_square - along_vector * along_vector / norm_vector
    corr_view = (orthogonal * lax.rsqrt(square_norm / entries + 1e-06)).astype(jnp.bfloat16)

    pairs_second = apply_partial(corr_view)
    mask_rows = lax.dynamic_slice_in_dim(own_mask, row_start, share_rows, 1)
    diag_rows = lax.dynamic_slice_in_dim(diag_view, row_start, share_rows, 1)
    corr_rows = lax.dynamic_slice_in_dim(corr_view, row_start, share_rows, 1).astype(jnp.float32)
    vector_rows = lax.dynamic_slice_in_dim(vector_view, row_start, share_rows, 1)
    product_rows = jnp.where(mask_rows, diag_rows * corr_rows + pairs_second, 0.0)
    local_terms = jnp.stack(
        [jnp.sum(vector_rows * product_rows), jnp.sum(corr_rows * product_rows)]
    )
    cross_term, self_term = reduce_vector(reduce_vector(local_terms, "op", n_op), "sec", n_sec)
    projected = jnp.stack(
        [rayleigh, cross_term * lax.rsqrt(norm_vector * entries), self_term / entries]
    )
    return (corr_view, product_rows, projected)


def solution(mesh):
    in_specs = (
        P("sec", None, None),
        P("sec", None, None),
        P("sec", None, None),
        P(("sec", "op"), None, None),
        P(("sec", "op"), None, None),
        P(("sec", "op")),
        P(("sec", "op")),
        P(("sec", "op")),
        P(),
        P(),
    )
    out_specs = (P("sec", None, None), P("sec", "op", None), P())
    return jax.shard_map(
        on_device, mesh=mesh, in_specs=in_specs, out_specs=out_specs, check_vma=False
    )
```

```python
import functools

import jax
import jax.numpy as jnp
from jax import lax
from jax.experimental import pallas as pl
from jax.experimental.pallas import tpu as pltpu
from jax.sharding import Mesh, PartitionSpec as P


def block_mask(left_dims, right_dims, block_size):
    positions = jnp.arange(block_size, dtype=jnp.int32)
    return (positions[None, :, None] < left_dims[:, None, None]) & (
        positions[None, None, :] < right_dims[:, None, None]
    )


SEC = ("chip", "core")


def gather_sec(value, chips):
    spread = jnp.broadcast_to(value[None], (chips,) + value.shape)
    same_core = lax.all_to_all(spread, "chip", 0, 0, tiled=True)
    other_core = lax.ppermute(same_core, "core", [(0, 1), (1, 0)])
    return jnp.concatenate([same_core, other_core], 0)


def ordered_gather(value, axis_name, count):
    spread = jnp.broadcast_to(value[None], (count,) + value.shape)
    return lax.all_to_all(spread, axis_name, 0, 0, tiled=True)


def reduce_vector(values, axis_name, count):
    return jnp.sum(ordered_gather(values, axis_name, count), axis=0)


def reduce_scatter_rows(partial_value, axis_name, count):
    sectors, rows, cols = partial_value.shape
    chunks = partial_value.reshape((sectors, count, rows // count, cols)).transpose(1, 0, 2, 3)
    received = lax.all_to_all(chunks, axis_name, 0, 0, tiled=True)
    return jnp.sum(received, axis=0)


def pair_kernel(src_ref, tgt_ref, cnt_ref, s_ref, l_ref, r_ref, o_ref):
    k = pl.program_id(0)

    @pl.when(k == 0)
    def _():
        o_ref[...] = jnp.zeros_like(o_ref)

    @pl.when(k < cnt_ref[0])
    def _():
        middle = jnp.dot(l_ref[0], s_ref[0], preferred_element_type=jnp.float32)
        high = middle.astype(jnp.bfloat16)
        low = (middle - high.astype(jnp.float32)).astype(jnp.bfloat16)
        right = r_ref[0]
        contribution = jnp.dot(high, right, preferred_element_type=jnp.float32) + jnp.dot(
            low, right, preferred_element_type=jnp.float32
        )
        t = tgt_ref[k]
        o_ref[t] = o_ref[t] + contribution


def pair_partial(sources, left_blocks, right_blocks, source_index, target_index, live_count, sector_count):
    slots, block_size, _ = left_blocks.shape
    n_sources = sources.shape[0]

    def live_slot(k, cnt):
        return jnp.minimum(k, jnp.clip(cnt[0] - 1, 0, slots - 1))

    def source_map(k, src, tgt, cnt):
        return (jnp.clip(src[live_slot(k, cnt)], 0, n_sources - 1), 0, 0)

    def operator_map(k, src, tgt, cnt):
        return (live_slot(k, cnt), 0, 0)

    block = (1, block_size, block_size)
    grid_spec = pltpu.PrefetchScalarGridSpec(
        num_scalar_prefetch=3,
        grid=(slots,),
        in_specs=[
            pl.BlockSpec(block, source_map),
            pl.BlockSpec(block, operator_map),
            pl.BlockSpec(block, operator_map),
        ],
        out_specs=pl.BlockSpec(
            (sector_count, block_size, block_size), lambda k, src, tgt, cnt: (0, 0, 0)
        ),
    )
    return pl.pallas_call(
        pair_kernel,
        grid_spec=grid_spec,
        out_shape=jax.ShapeDtypeStruct((sector_count, block_size, block_size), jnp.float32),
        compiler_params=pltpu.CompilerParams(dimension_semantics=("arbitrary",)),
    )(source_index, target_index, live_count, sources, left_blocks, right_blocks)


def on_device(
    wavefunction,
    diagonal,
    preconditioner,
    left_operator_blocks,
    right_operator_blocks,
    slot_source_sector,
    slot_target_sector,
    pair_count,
    left_dims,
    right_dims,
):
    sector_count = wavefunction.shape[0]
    block_size = wavefunction.shape[1]
    n_chip = lax.axis_size("chip")
    n_sec = n_chip * lax.axis_size("core")
    n_op = lax.axis_size("op")
    share_rows = block_size // n_op
    sec_index = lax.axis_index(SEC)
    core_index = lax.axis_index("core")
    op_index = lax.axis_index("op")
    first_sector = sec_index * sector_count
    row_start = op_index * share_rows
    entries = float(left_dims.shape[0] * block_size * block_size)
    own_mask = block_mask(
        lax.dynamic_slice_in_dim(left_dims, first_sector, sector_count),
        lax.dynamic_slice_in_dim(right_dims, first_sector, sector_count),
        block_size,
    )
    own_vector = jnp.where(own_mask, wavefunction, jnp.zeros_like(wavefunction))
    diag_view = diagonal.astype(jnp.float32)
    scale_view = preconditioner.astype(jnp.float32)
    vector_view = own_vector.astype(jnp.float32)

    owner = slot_source_sector // sector_count
    owner_core = owner % 2
    position = (owner_core != core_index).astype(jnp.int32) * n_chip + owner // 2
    source_index = position * sector_count + slot_source_sector % sector_count
    target_index = jnp.clip(slot_target_sector, 0, sector_count - 1)
    live_count = pair_count

    def apply_partial(field):
        sources = gather_sec(field, n_chip).reshape(
            (n_sec * sector_count, block_size, block_size)
        )
        partial_value = pair_partial(
            sources,
            left_operator_blocks,
            right_operator_blocks,
            source_index,
            target_index,
            live_count,
            sector_count,
        )
        return reduce_scatter_rows(partial_value, "op", n_op)

    pair_rows = apply_partial(own_vector)
    pairs_first = (
        ordered_gather(pair_rows, "op", n_op)
        .transpose(1, 0, 2, 3)
        .reshape((sector_count, block_size, block_size))
    )
    sigma_first = jnp.where(own_mask, diag_view * vector_view + pairs_first, 0.0)
    norm_vector, correlation = reduce_vector(
        jnp.stack([jnp.sum(vector_view * vector_view), jnp.sum(vector_view * sigma_first)]),
        SEC,
        n_sec,
    )
    rayleigh = correlation / norm_vector
    residual = sigma_first - rayleigh * vector_view
    scaled = scale_view * residual
    along_vector, scaled_square = reduce_vector(
        jnp.stack([jnp.sum(vector_view * scaled), jnp.sum(scaled * scaled)]), SEC, n_sec
    )
    orthogonal = scaled - along_vector / norm_vector * vector_view
    square_norm = scaled_square - along_vector * along_vector / norm_vector
    corr_view = (orthogonal * lax.rsqrt(square_norm / entries + 1e-06)).astype(jnp.bfloat16)

    pairs_second = apply_partial(corr_view)
    mask_rows = lax.dynamic_slice_in_dim(own_mask, row_start, share_rows, 1)
    diag_rows = lax.dynamic_slice_in_dim(diag_view, row_start, share_rows, 1)
    corr_rows = lax.dynamic_slice_in_dim(corr_view, row_start, share_rows, 1).astype(jnp.float32)
    vector_rows = lax.dynamic_slice_in_dim(vector_view, row_start, share_rows, 1)
    product_rows = jnp.where(mask_rows, diag_rows * corr_rows + pairs_second, 0.0)
    local_terms = jnp.stack(
        [jnp.sum(vector_rows * product_rows), jnp.sum(corr_rows * product_rows)]
    )
    cross_term, self_term = reduce_vector(reduce_vector(local_terms, "op", n_op), SEC, n_sec)
    projected = jnp.stack(
        [rayleigh, cross_term * lax.rsqrt(norm_vector * entries), self_term / entries]
    )
    return (corr_view, product_rows, projected)


def solution(mesh):
    n_sec, n_op = mesh.devices.shape
    mesh = Mesh(mesh.devices.reshape((n_sec // 2, 2, n_op)), ("chip", "core", "op"))
    in_specs = (
        P(SEC, None, None),
        P(SEC, None, None),
        P(SEC, None, None),
        P(("chip", "core", "op"), None, None),
        P(("chip", "core", "op"), None, None),
        P(("chip", "core", "op")),
        P(("chip", "core", "op")),
        P(("chip", "core", "op")),
        P(),
        P(),
    )
    out_specs = (P(SEC, None, None), P(SEC, "op", None), P())
    return jax.shard_map(
        on_device, mesh=mesh, in_specs=in_specs, out_specs=out_specs, check_vma=False
    )
```

```python
import functools

import jax
import jax.numpy as jnp
from jax import lax
from jax.experimental import pallas as pl
from jax.experimental.pallas import tpu as pltpu
from jax.sharding import Mesh, PartitionSpec as P


def block_mask(left_dims, right_dims, block_size):
    positions = jnp.arange(block_size, dtype=jnp.int32)
    return (positions[None, :, None] < left_dims[:, None, None]) & (
        positions[None, None, :] < right_dims[:, None, None]
    )


SEC = ("chip", "core")
OP = ("z", "xl")


def gather_sec(value, chips):
    spread = jnp.broadcast_to(value[None], (chips,) + value.shape)
    same_core = lax.all_to_all(spread, "chip", 0, 0, tiled=True)
    other_core = lax.ppermute(same_core, "core", [(0, 1), (1, 0)])
    return jnp.concatenate([same_core, other_core], 0)


def ordered_gather(value, axis_name, count):
    spread = jnp.broadcast_to(value[None], (count,) + value.shape)
    return lax.all_to_all(spread, axis_name, 0, 0, tiled=True)


def reduce_vector(values, axis_name, count):
    return jnp.sum(ordered_gather(values, axis_name, count), axis=0)


def reduce_scatter_rows(partial_value, extra, zs):
    sectors, rows, cols = partial_value.shape
    share = rows // (2 * zs)
    chunks = partial_value.reshape((sectors, zs, 2, share, cols)).transpose(2, 1, 0, 3, 4)
    chunks = chunks.reshape((2, zs, sectors * share * cols))
    tail = jnp.zeros((2, zs, 128), jnp.float32).at[:, :, : extra.shape[0]].set(extra)
    chunks = jnp.concatenate([chunks, tail], axis=2)
    xl = lax.axis_index("xl")
    mine = lax.dynamic_index_in_dim(chunks, xl, 0, keepdims=False)
    other = lax.dynamic_index_in_dim(chunks, 1 - xl, 0, keepdims=False)
    pair_sum = mine + lax.ppermute(other, "xl", [(0, 1), (1, 0)])
    total = jnp.sum(lax.all_to_all(pair_sum, "z", 0, 0, tiled=True), axis=0)
    body = total[: sectors * share * cols].reshape((sectors, share, cols))
    return body, total[sectors * share * cols : sectors * share * cols + extra.shape[0]]


def gather_rows(rows_value, zs):
    sectors, share, cols = rows_value.shape
    spread = jnp.broadcast_to(rows_value[None], (zs,) + rows_value.shape)
    same = lax.all_to_all(spread, "z", 0, 0, tiled=True)
    other = lax.ppermute(same, "xl", [(0, 1), (1, 0)])
    xl = lax.axis_index("xl")
    pair = jnp.where(xl == 0, jnp.stack([same, other], 1), jnp.stack([other, same], 1))
    return pair.reshape((2 * zs, sectors, share, cols)).transpose(1, 0, 2, 3).reshape(
        (sectors, 2 * zs * share, cols)
    )


def pair_kernel(src_ref, tgt_ref, cnt_ref, s_ref, l_ref, r_ref, o_ref):
    k = pl.program_id(0)

    @pl.when(k == 0)
    def _():
        o_ref[...] = jnp.zeros_like(o_ref)

    @pl.when(k < cnt_ref[0])
    def _():
        middle = jnp.dot(l_ref[0], s_ref[0], preferred_element_type=jnp.float32)
        high = middle.astype(jnp.bfloat16)
        low = (middle - high.astype(jnp.float32)).astype(jnp.bfloat16)
        right = r_ref[0]
        contribution = jnp.dot(high, right, preferred_element_type=jnp.float32) + jnp.dot(
            low, right, preferred_element_type=jnp.float32
        )
        t = tgt_ref[k]
        o_ref[t] = o_ref[t] + contribution


def pair_partial(sources, left_blocks, right_blocks, source_index, target_index, live_count, sector_count):
    slots, block_size, _ = left_blocks.shape
    n_sources = sources.shape[0]

    def live_slot(k, cnt):
        return jnp.minimum(k, jnp.clip(cnt[0] - 1, 0, slots - 1))

    def source_map(k, src, tgt, cnt):
        return (jnp.clip(src[live_slot(k, cnt)], 0, n_sources - 1), 0, 0)

    def operator_map(k, src, tgt, cnt):
        return (live_slot(k, cnt), 0, 0)

    block = (1, block_size, block_size)
    grid_spec = pltpu.PrefetchScalarGridSpec(
        num_scalar_prefetch=3,
        grid=(slots,),
        in_specs=[
            pl.BlockSpec(block, source_map),
            pl.BlockSpec(block, operator_map),
            pl.BlockSpec(block, operator_map),
        ],
        out_specs=pl.BlockSpec(
            (sector_count, block_size, block_size), lambda k, src, tgt, cnt: (0, 0, 0)
        ),
    )
    return pl.pallas_call(
        pair_kernel,
        grid_spec=grid_spec,
        out_shape=jax.ShapeDtypeStruct((sector_count, block_size, block_size), jnp.float32),
        compiler_params=pltpu.CompilerParams(dimension_semantics=("arbitrary",)),
    )(source_index, target_index, live_count, sources, left_blocks, right_blocks)


def on_device(
    wavefunction,
    diagonal,
    preconditioner,
    left_operator_blocks,
    right_operator_blocks,
    slot_source_sector,
    slot_target_sector,
    pair_count,
    left_dims,
    right_dims,
):
    sector_count = wavefunction.shape[0]
    block_size = wavefunction.shape[1]
    n_chip = lax.axis_size("chip")
    n_sec = n_chip * lax.axis_size("core")
    n_z = lax.axis_size("z")
    n_op = n_z * lax.axis_size("xl")
    share_rows = block_size // n_op
    sec_index = lax.axis_index(SEC)
    core_index = lax.axis_index("core")
    op_index = lax.axis_index(OP)
    first_sector = sec_index * sector_count
    row_start = op_index * share_rows
    entries = float(left_dims.shape[0] * block_size * block_size)
    own_mask = block_mask(
        lax.dynamic_slice_in_dim(left_dims, first_sector, sector_count),
        lax.dynamic_slice_in_dim(right_dims, first_sector, sector_count),
        block_size,
    )
    own_vector = jnp.where(own_mask, wavefunction, jnp.zeros_like(wavefunction))
    diag_view = diagonal.astype(jnp.float32)
    scale_view = preconditioner.astype(jnp.float32)
    vector_view = own_vector.astype(jnp.float32)

    owner = slot_source_sector // sector_count
    owner_core = owner % 2
    position = (owner_core != core_index).astype(jnp.int32) * n_chip + owner // 2
    source_index = position * sector_count + slot_source_sector % sector_count
    target_index = jnp.clip(slot_target_sector, 0, sector_count - 1)
    live_count = pair_count

    def apply_partial(field, weights):
        sources = gather_sec(field, n_chip).reshape(
            (n_sec * sector_count, block_size, block_size)
        )
        partial_value = pair_partial(
            sources,
            left_operator_blocks,
            right_operator_blocks,
            source_index,
            target_index,
            live_count,
            sector_count,
        )
        extra = jnp.stack([jnp.sum(w * partial_value) for w in weights] or [jnp.float32(0)])
        return reduce_scatter_rows(partial_value, extra, n_z)

    pair_rows, _ = apply_partial(own_vector, ())
    pairs_first = gather_rows(pair_rows, n_z)
    sigma_first = jnp.where(own_mask, diag_view * vector_view + pairs_first, 0.0)
    norm_vector, correlation = reduce_vector(
        jnp.stack([jnp.sum(vector_view * vector_view), jnp.sum(vector_view * sigma_first)]),
        SEC,
        n_sec,
    )
    rayleigh = correlation / norm_vector
    residual = sigma_first - rayleigh * vector_view
    scaled = scale_view * residual
    along_vector, scaled_square = reduce_vector(
        jnp.stack([jnp.sum(vector_view * scaled), jnp.sum(scaled * scaled)]), SEC, n_sec
    )
    orthogonal = scaled - along_vector / norm_vector * vector_view
    square_norm = scaled_square - along_vector * along_vector / norm_vector
    corr_view = (orthogonal * lax.rsqrt(square_norm / entries + 1e-06)).astype(jnp.bfloat16)

    corr_full = corr_view.astype(jnp.float32)
    pairs_second, pair_terms = apply_partial(corr_view, (vector_view, corr_full))
    mask_rows = lax.dynamic_slice_in_dim(own_mask, row_start, share_rows, 1)
    diag_rows = lax.dynamic_slice_in_dim(diag_view, row_start, share_rows, 1)
    corr_rows = lax.dynamic_slice_in_dim(corr_view, row_start, share_rows, 1).astype(jnp.float32)
    product_rows = jnp.where(mask_rows, diag_rows * corr_rows + pairs_second, 0.0)
    local_terms = jnp.stack(
        [jnp.sum(vector_view * diag_view * corr_full), jnp.sum(corr_full * diag_view * corr_full)]
    )
    cross_term, self_term = reduce_vector(local_terms + pair_terms, SEC, n_sec)
    projected = jnp.stack(
        [rayleigh, cross_term * lax.rsqrt(norm_vector * entries), self_term / entries]
    )
    return (corr_view, product_rows, projected)


def solution(mesh):
    n_sec, n_op = mesh.devices.shape
    mesh = Mesh(mesh.devices.reshape((n_sec // 2, 2, n_op // 2, 2)), ("chip", "core", "z", "xl"))
    in_specs = (
        P(SEC, None, None),
        P(SEC, None, None),
        P(SEC, None, None),
        P(("chip", "core", "z", "xl"), None, None),
        P(("chip", "core", "z", "xl"), None, None),
        P(("chip", "core", "z", "xl")),
        P(("chip", "core", "z", "xl")),
        P(("chip", "core", "z", "xl")),
        P(),
        P(),
    )
    out_specs = (P(SEC, None, None), P(SEC, OP, None), P())
    return jax.shard_map(
        on_device, mesh=mesh, in_specs=in_specs, out_specs=out_specs, check_vma=False
    )
```

```python
import functools

import jax
import jax.numpy as jnp
from jax import lax
from jax.experimental import pallas as pl
from jax.experimental.pallas import tpu as pltpu
from jax.sharding import Mesh, PartitionSpec as P


def block_mask(left_dims, right_dims, block_size):
    positions = jnp.arange(block_size, dtype=jnp.int32)
    return (positions[None, :, None] < left_dims[:, None, None]) & (
        positions[None, None, :] < right_dims[:, None, None]
    )


SEC = ("chip", "core")
OP = ("z", "xl")


def gather_sec(value, chips):
    spread = jnp.broadcast_to(value[None], (chips,) + value.shape)
    same_core = lax.all_to_all(spread, "chip", 0, 0, tiled=True)
    other_core = lax.ppermute(same_core, "core", [(0, 1), (1, 0)])
    return same_core, other_core


def ordered_gather(value, axis_name, count):
    spread = jnp.broadcast_to(value[None], (count,) + value.shape)
    return lax.all_to_all(spread, axis_name, 0, 0, tiled=True)


def reduce_vector(values, axis_name, count):
    return jnp.sum(ordered_gather(values, axis_name, count), axis=0)


def reduce_scatter_rows(partial_value, extra, zs):
    sectors, rows, cols = partial_value.shape
    share = rows // (2 * zs)
    chunks = partial_value.reshape((sectors, zs, 2, share, cols)).transpose(2, 1, 0, 3, 4)
    chunks = chunks.reshape((2, zs, sectors * share * cols))
    tail = jnp.zeros((2, zs, 128), jnp.float32).at[:, :, : extra.shape[0]].set(extra)
    chunks = jnp.concatenate([chunks, tail], axis=2)
    xl = lax.axis_index("xl")
    mine = lax.dynamic_index_in_dim(chunks, xl, 0, keepdims=False)
    other = lax.dynamic_index_in_dim(chunks, 1 - xl, 0, keepdims=False)
    pair_sum = mine + lax.ppermute(other, "xl", [(0, 1), (1, 0)])
    total = jnp.sum(lax.all_to_all(pair_sum, "z", 0, 0, tiled=True), axis=0)
    body = total[: sectors * share * cols].reshape((sectors, share, cols))
    return body, total[sectors * share * cols : sectors * share * cols + extra.shape[0]]


def gather_rows(rows_value, zs):
    sectors, share, cols = rows_value.shape
    spread = jnp.broadcast_to(rows_value[None], (zs,) + rows_value.shape)
    same = lax.all_to_all(spread, "z", 0, 0, tiled=True)
    other = lax.ppermute(same, "xl", [(0, 1), (1, 0)])
    xl = lax.axis_index("xl")
    pair = jnp.where(xl == 0, jnp.stack([same, other], 1), jnp.stack([other, same], 1))
    return pair.reshape((2 * zs, sectors, share, cols)).transpose(1, 0, 2, 3).reshape(
        (sectors, 2 * zs * share, cols)
    )


def pair_kernel(same_idx, other_idx, side_ref, tgt_ref, cnt_ref, a_ref, b_ref, l_ref, r_ref, o_ref):
    k = pl.program_id(0)

    @pl.when(k == 0)
    def _():
        o_ref[...] = jnp.zeros_like(o_ref)

    def add_pair(s_ref):
        middle = jnp.dot(l_ref[0], s_ref[0], preferred_element_type=jnp.float32)
        high = middle.astype(jnp.bfloat16)
        low = (middle - high.astype(jnp.float32)).astype(jnp.bfloat16)
        right = r_ref[0]
        contribution = jnp.dot(high, right, preferred_element_type=jnp.float32) + jnp.dot(
            low, right, preferred_element_type=jnp.float32
        )
        t = tgt_ref[k]
        o_ref[t] = o_ref[t] + contribution

    live = k < cnt_ref[0]

    @pl.when(live & (side_ref[k] == 0))
    def _():
        add_pair(a_ref)

    @pl.when(live & (side_ref[k] != 0))
    def _():
        add_pair(b_ref)


def carried(index, used):
    slots = index.shape[0]
    order = jnp.arange(slots, dtype=jnp.int32)
    last = lax.cummax(jnp.where(used, order, -1), axis=0)
    first = jnp.argmax(used).astype(jnp.int32)
    return index[jnp.where(last < 0, first, last)]


def pair_partial(sources, left_blocks, right_blocks, source_index, target_index, live_count, sector_count):
    same_core, other_core = sources
    slots, block_size, _ = left_blocks.shape
    chips = same_core.shape[0]
    same_core = same_core.reshape((chips * sector_count, block_size, block_size))
    other_core = other_core.reshape((chips * sector_count, block_size, block_size))
    last_live = jnp.clip(live_count[0] - 1, 0, slots - 1)
    slot_ids = jnp.minimum(jnp.arange(slots, dtype=jnp.int32), last_live)
    wanted = jnp.clip(source_index[slot_ids], 0, 2 * chips * sector_count - 1)
    side = (wanted >= chips * sector_count).astype(jnp.int32)
    within = wanted - side * chips * sector_count
    same_idx = carried(within, side == 0)
    other_idx = carried(within, side != 0)
    target = target_index[slot_ids]

    def same_map(k, a, b, sd, tg, cnt):
        return (a[k], 0, 0)

    def other_map(k, a, b, sd, tg, cnt):
        return (b[k], 0, 0)

    def operator_map(k, a, b, sd, tg, cnt):
        return (jnp.minimum(k, jnp.clip(cnt[0] - 1, 0, slots - 1)), 0, 0)

    block = (1, block_size, block_size)
    grid_spec = pltpu.PrefetchScalarGridSpec(
        num_scalar_prefetch=5,
        grid=(slots,),
        in_specs=[
            pl.BlockSpec(block, same_map),
            pl.BlockSpec(block, other_map),
            pl.BlockSpec(block, operator_map),
            pl.BlockSpec(block, operator_map),
        ],
        out_specs=pl.BlockSpec(
            (sector_count, block_size, block_size), lambda k, a, b, sd, tg, cnt: (0, 0, 0)
        ),
    )
    return pl.pallas_call(
        pair_kernel,
        grid_spec=grid_spec,
        out_shape=jax.ShapeDtypeStruct((sector_count, block_size, block_size), jnp.float32),
        compiler_params=pltpu.CompilerParams(dimension_semantics=("arbitrary",)),
    )(same_idx, other_idx, side, target, live_count, same_core, other_core, left_blocks, right_blocks)


def on_device(
    wavefunction,
    diagonal,
    preconditioner,
    left_operator_blocks,
    right_operator_blocks,
    slot_source_sector,
    slot_target_sector,
    pair_count,
    left_dims,
    right_dims,
):
    sector_count = wavefunction.shape[0]
    block_size = wavefunction.shape[1]
    n_chip = lax.axis_size("chip")
    n_sec = n_chip * lax.axis_size("core")
    n_z = lax.axis_size("z")
    n_op = n_z * lax.axis_size("xl")
    share_rows = block_size // n_op
    sec_index = lax.axis_index(SEC)
    core_index = lax.axis_index("core")
    op_index = lax.axis_index(OP)
    first_sector = sec_index * sector_count
    row_start = op_index * share_rows
    entries = float(left_dims.shape[0] * block_size * block_size)
    own_mask = block_mask(
        lax.dynamic_slice_in_dim(left_dims, first_sector, sector_count),
        lax.dynamic_slice_in_dim(right_dims, first_sector, sector_count),
        block_size,
    )
    own_vector = jnp.where(own_mask, wavefunction, jnp.zeros_like(wavefunction))
    diag_view = diagonal.astype(jnp.float32)
    scale_view = preconditioner.astype(jnp.float32)
    vector_view = own_vector.astype(jnp.float32)

    owner = slot_source_sector // sector_count
    owner_core = owner % 2
    position = (owner_core != core_index).astype(jnp.int32) * n_chip + owner // 2
    source_index = position * sector_count + slot_source_sector % sector_count
    target_index = jnp.clip(slot_target_sector, 0, sector_count - 1)
    live_count = pair_count

    def apply_partial(field, weights):
        sources = gather_sec(field, n_chip)
        partial_value = pair_partial(
            sources,
            left_operator_blocks,
            right_operator_blocks,
            source_index,
            target_index,
            live_count,
            sector_count,
        )
        extra = jnp.stack([jnp.sum(w * partial_value) for w in weights] or [jnp.float32(0)])
        return reduce_scatter_rows(partial_value, extra, n_z)

    pair_rows, _ = apply_partial(own_vector, ())
    pairs_first = gather_rows(pair_rows, n_z)
    sigma_first = jnp.where(own_mask, diag_view * vector_view + pairs_first, 0.0)
    norm_vector, correlation = reduce_vector(
        jnp.stack([jnp.sum(vector_view * vector_view), jnp.sum(vector_view * sigma_first)]),
        SEC,
        n_sec,
    )
    rayleigh = correlation / norm_vector
    residual = sigma_first - rayleigh * vector_view
    scaled = scale_view * residual
    along_vector, scaled_square = reduce_vector(
        jnp.stack([jnp.sum(vector_view * scaled), jnp.sum(scaled * scaled)]), SEC, n_sec
    )
    orthogonal = scaled - along_vector / norm_vector * vector_view
    square_norm = scaled_square - along_vector * along_vector / norm_vector
    corr_view = (orthogonal * lax.rsqrt(square_norm / entries + 1e-06)).astype(jnp.bfloat16)

    corr_full = corr_view.astype(jnp.float32)
    pairs_second, pair_terms = apply_partial(corr_view, (vector_view, corr_full))
    mask_rows = lax.dynamic_slice_in_dim(own_mask, row_start, share_rows, 1)
    diag_rows = lax.dynamic_slice_in_dim(diag_view, row_start, share_rows, 1)
    corr_rows = lax.dynamic_slice_in_dim(corr_view, row_start, share_rows, 1).astype(jnp.float32)
    product_rows = jnp.where(mask_rows, diag_rows * corr_rows + pairs_second, 0.0)
    local_terms = jnp.stack(
        [jnp.sum(vector_view * diag_view * corr_full), jnp.sum(corr_full * diag_view * corr_full)]
    )
    cross_term, self_term = reduce_vector(local_terms + pair_terms, SEC, n_sec)
    projected = jnp.stack(
        [rayleigh, cross_term * lax.rsqrt(norm_vector * entries), self_term / entries]
    )
    return (corr_view, product_rows, projected)


def solution(mesh):
    n_sec, n_op = mesh.devices.shape
    mesh = Mesh(mesh.devices.reshape((n_sec // 2, 2, n_op // 2, 2)), ("chip", "core", "z", "xl"))
    in_specs = (
        P(SEC, None, None),
        P(SEC, None, None),
        P(SEC, None, None),
        P(("chip", "core", "z", "xl"), None, None),
        P(("chip", "core", "z", "xl"), None, None),
        P(("chip", "core", "z", "xl")),
        P(("chip", "core", "z", "xl")),
        P(("chip", "core", "z", "xl")),
        P(),
        P(),
    )
    out_specs = (P(SEC, None, None), P(SEC, OP, None), P())
    return jax.shard_map(
        on_device, mesh=mesh, in_specs=in_specs, out_specs=out_specs, check_vma=False
    )
```

```python
import functools

import jax
import jax.numpy as jnp
from jax import lax
from jax.experimental import pallas as pl
from jax.experimental.pallas import tpu as pltpu
from jax.sharding import Mesh, PartitionSpec as P


def block_mask(left_dims, right_dims, block_size):
    positions = jnp.arange(block_size, dtype=jnp.int32)
    return (positions[None, :, None] < left_dims[:, None, None]) & (
        positions[None, None, :] < right_dims[:, None, None]
    )


SEC = ("chip", "core")
OP = ("z", "xl")


def gather_sec(value, chips):
    spread = jnp.broadcast_to(value[None], (chips,) + value.shape)
    same_core = lax.all_to_all(spread, "chip", 0, 0, tiled=True)
    other_core = lax.ppermute(same_core, "core", [(0, 1), (1, 0)])
    return same_core, other_core


def ordered_gather(value, axis_name, count):
    spread = jnp.broadcast_to(value[None], (count,) + value.shape)
    return lax.all_to_all(spread, axis_name, 0, 0, tiled=True)


def reduce_vector(values, axis_name, count):
    return jnp.sum(ordered_gather(values, axis_name, count), axis=0)


def reduce_scatter_rows(partial_value, extra, zs):
    sectors, rows, cols = partial_value.shape
    share = rows // (2 * zs)
    chunks = partial_value.reshape((sectors, zs, 2, share, cols)).transpose(2, 1, 0, 3, 4)
    chunks = chunks.reshape((2, zs, sectors * share * cols))
    tail = jnp.zeros((2, zs, 128), jnp.float32).at[:, :, : extra.shape[0]].set(extra)
    chunks = jnp.concatenate([chunks, tail], axis=2)
    xl = lax.axis_index("xl")
    mine = lax.dynamic_index_in_dim(chunks, xl, 0, keepdims=False)
    other = lax.dynamic_index_in_dim(chunks, 1 - xl, 0, keepdims=False)
    pair_sum = mine + lax.ppermute(other, "xl", [(0, 1), (1, 0)])
    total = jnp.sum(lax.all_to_all(pair_sum, "z", 0, 0, tiled=True), axis=0)
    body = total[: sectors * share * cols].reshape((sectors, share, cols))
    return body, total[sectors * share * cols : sectors * share * cols + extra.shape[0]]


def gather_rows(rows_value, zs):
    sectors, share, cols = rows_value.shape
    spread = jnp.broadcast_to(rows_value[None], (zs,) + rows_value.shape)
    same = lax.all_to_all(spread, "z", 0, 0, tiled=True)
    other = lax.ppermute(same, "xl", [(0, 1), (1, 0)])
    xl = lax.axis_index("xl")
    pair = jnp.where(xl == 0, jnp.stack([same, other], 1), jnp.stack([other, same], 1))
    return pair.reshape((2 * zs, sectors, share, cols)).transpose(1, 0, 2, 3).reshape(
        (sectors, 2 * zs * share, cols)
    )


def pair_kernel(same_idx, other_idx, side_ref, tgt_ref, cnt_ref, a_ref, b_ref, l_ref, r_ref, o_ref):
    k = pl.program_id(0)

    @pl.when(k == 0)
    def _():
        o_ref[...] = jnp.zeros_like(o_ref)

    @pl.when(k < cnt_ref[0])
    def _():
        source = jnp.where(side_ref[k] == 0, a_ref[0], b_ref[0])
        middle = jnp.dot(l_ref[0], source, preferred_element_type=jnp.float32)
        high = middle.astype(jnp.bfloat16)
        low = (middle - high.astype(jnp.float32)).astype(jnp.bfloat16)
        right = r_ref[0]
        contribution = jnp.dot(high, right, preferred_element_type=jnp.float32) + jnp.dot(
            low, right, preferred_element_type=jnp.float32
        )
        t = tgt_ref[k]
        o_ref[t] = o_ref[t] + contribution


def carried(index, used):
    slots = index.shape[0]
    order = jnp.arange(slots, dtype=jnp.int32)
    last = lax.cummax(jnp.where(used, order, -1), axis=0)
    first = jnp.argmax(used).astype(jnp.int32)
    return index[jnp.where(last < 0, first, last)]


def pair_partial(sources, left_blocks, right_blocks, source_index, target_index, live_count, sector_count):
    same_core, other_core = sources
    slots, block_size, _ = left_blocks.shape
    chips = same_core.shape[0]
    same_core = same_core.reshape((chips * sector_count, block_size, block_size))
    other_core = other_core.reshape((chips * sector_count, block_size, block_size))
    last_live = jnp.clip(live_count[0] - 1, 0, slots - 1)
    slot_ids = jnp.minimum(jnp.arange(slots, dtype=jnp.int32), last_live)
    wanted = jnp.clip(source_index[slot_ids], 0, 2 * chips * sector_count - 1)
    side = (wanted >= chips * sector_count).astype(jnp.int32)
    within = wanted - side * chips * sector_count
    same_idx = carried(within, side == 0)
    other_idx = carried(within, side != 0)
    target = target_index[slot_ids]

    def same_map(k, a, b, sd, tg, cnt):
        return (a[k], 0, 0)

    def other_map(k, a, b, sd, tg, cnt):
        return (b[k], 0, 0)

    def operator_map(k, a, b, sd, tg, cnt):
        return (jnp.minimum(k, jnp.clip(cnt[0] - 1, 0, slots - 1)), 0, 0)

    block = (1, block_size, block_size)
    grid_spec = pltpu.PrefetchScalarGridSpec(
        num_scalar_prefetch=5,
        grid=(slots,),
        in_specs=[
            pl.BlockSpec(block, same_map),
            pl.BlockSpec(block, other_map),
            pl.BlockSpec(block, operator_map),
            pl.BlockSpec(block, operator_map),
        ],
        out_specs=pl.BlockSpec(
            (sector_count, block_size, block_size), lambda k, a, b, sd, tg, cnt: (0, 0, 0)
        ),
    )
    return pl.pallas_call(
        pair_kernel,
        grid_spec=grid_spec,
        out_shape=jax.ShapeDtypeStruct((sector_count, block_size, block_size), jnp.float32),
        compiler_params=pltpu.CompilerParams(dimension_semantics=("arbitrary",)),
    )(same_idx, other_idx, side, target, live_count, same_core, other_core, left_blocks, right_blocks)


def on_device(
    wavefunction,
    diagonal,
    preconditioner,
    left_operator_blocks,
    right_operator_blocks,
    slot_source_sector,
    slot_target_sector,
    pair_count,
    left_dims,
    right_dims,
):
    sector_count = wavefunction.shape[0]
    block_size = wavefunction.shape[1]
    n_chip = lax.axis_size("chip")
    n_sec = n_chip * lax.axis_size("core")
    n_z = lax.axis_size("z")
    n_op = n_z * lax.axis_size("xl")
    share_rows = block_size // n_op
    sec_index = lax.axis_index(SEC)
    core_index = lax.axis_index("core")
    op_index = lax.axis_index(OP)
    first_sector = sec_index * sector_count
    row_start = op_index * share_rows
    entries = float(left_dims.shape[0] * block_size * block_size)
    own_mask = block_mask(
        lax.dynamic_slice_in_dim(left_dims, first_sector, sector_count),
        lax.dynamic_slice_in_dim(right_dims, first_sector, sector_count),
        block_size,
    )
    own_vector = jnp.where(own_mask, wavefunction, jnp.zeros_like(wavefunction))
    diag_view = diagonal.astype(jnp.float32)
    scale_view = preconditioner.astype(jnp.float32)
    vector_view = own_vector.astype(jnp.float32)

    owner = slot_source_sector // sector_count
    owner_core = owner % 2
    position = (owner_core != core_index).astype(jnp.int32) * n_chip + owner // 2
    source_index = position * sector_count + slot_source_sector % sector_count
    target_index = jnp.clip(slot_target_sector, 0, sector_count - 1)
    live_count = pair_count

    def apply_partial(field, weights):
        sources = gather_sec(field, n_chip)
        partial_value = pair_partial(
            sources,
            left_operator_blocks,
            right_operator_blocks,
            source_index,
            target_index,
            live_count,
            sector_count,
        )
        extra = jnp.stack([jnp.sum(w * partial_value) for w in weights] or [jnp.float32(0)])
        return reduce_scatter_rows(partial_value, extra, n_z)

    pair_rows, first_terms = apply_partial(own_vector, (vector_view,))
    norm_vector, correlation = reduce_vector(
        jnp.stack(
            [
                jnp.sum(vector_view * vector_view),
                jnp.sum(vector_view * diag_view * vector_view) + first_terms[0],
            ]
        ),
        SEC,
        n_sec,
    )
    pairs_first = gather_rows(pair_rows, n_z)
    sigma_first = jnp.where(own_mask, diag_view * vector_view + pairs_first, 0.0)
    rayleigh = correlation / norm_vector
    residual = sigma_first - rayleigh * vector_view
    scaled = scale_view * residual
    along_vector, scaled_square = reduce_vector(
        jnp.stack([jnp.sum(vector_view * scaled), jnp.sum(scaled * scaled)]), SEC, n_sec
    )
    orthogonal = scaled - along_vector / norm_vector * vector_view
    square_norm = scaled_square - along_vector * along_vector / norm_vector
    corr_view = (orthogonal * lax.rsqrt(square_norm / entries + 1e-06)).astype(jnp.bfloat16)

    corr_full = corr_view.astype(jnp.float32)
    pairs_second, pair_terms = apply_partial(corr_view, (vector_view, corr_full))
    mask_rows = lax.dynamic_slice_in_dim(own_mask, row_start, share_rows, 1)
    diag_rows = lax.dynamic_slice_in_dim(diag_view, row_start, share_rows, 1)
    corr_rows = lax.dynamic_slice_in_dim(corr_view, row_start, share_rows, 1).astype(jnp.float32)
    product_rows = jnp.where(mask_rows, diag_rows * corr_rows + pairs_second, 0.0)
    local_terms = jnp.stack(
        [jnp.sum(vector_view * diag_view * corr_full), jnp.sum(corr_full * diag_view * corr_full)]
    )
    cross_term, self_term = reduce_vector(local_terms + pair_terms, SEC, n_sec)
    projected = jnp.stack(
        [rayleigh, cross_term * lax.rsqrt(norm_vector * entries), self_term / entries]
    )
    return (corr_view, product_rows, projected)


def solution(mesh):
    n_sec, n_op = mesh.devices.shape
    mesh = Mesh(mesh.devices.reshape((n_sec // 2, 2, n_op // 2, 2)), ("chip", "core", "z", "xl"))
    in_specs = (
        P(SEC, None, None),
        P(SEC, None, None),
        P(SEC, None, None),
        P(("chip", "core", "z", "xl"), None, None),
        P(("chip", "core", "z", "xl"), None, None),
        P(("chip", "core", "z", "xl")),
        P(("chip", "core", "z", "xl")),
        P(("chip", "core", "z", "xl")),
        P(),
        P(),
    )
    out_specs = (P(SEC, None, None), P(SEC, OP, None), P())
    return jax.shard_map(
        on_device, mesh=mesh, in_specs=in_specs, out_specs=out_specs, check_vma=False
    )
```

```python
import functools

import jax
import jax.numpy as jnp
from jax import lax
from jax.experimental import pallas as pl
from jax.experimental.pallas import tpu as pltpu
from jax.sharding import Mesh, PartitionSpec as P


def block_mask(left_dims, right_dims, block_size):
    positions = jnp.arange(block_size, dtype=jnp.int32)
    return (positions[None, :, None] < left_dims[:, None, None]) & (
        positions[None, None, :] < right_dims[:, None, None]
    )


SEC = ("chip", "core")
OP = ("z", "xl")


def gather_sec(value, chips):
    spread = jnp.broadcast_to(value[None], (chips,) + value.shape)
    same_core = lax.all_to_all(spread, "chip", 0, 0, tiled=True)
    other_core = lax.ppermute(same_core, "core", [(0, 1), (1, 0)])
    return same_core, other_core


def ordered_gather(value, axis_name, count):
    spread = jnp.broadcast_to(value[None], (count,) + value.shape)
    return lax.all_to_all(spread, axis_name, 0, 0, tiled=True)


def reduce_vector(values, axis_name, count):
    return jnp.sum(ordered_gather(values, axis_name, count), axis=0)


def reduce_scatter_rows(partial_value, extra, zs):
    sectors, rows, cols = partial_value.shape
    share = rows // (2 * zs)
    chunks = partial_value.reshape((sectors, zs, 2, share, cols)).transpose(2, 1, 0, 3, 4)
    chunks = chunks.reshape((2, zs, sectors * share * cols))
    tail = jnp.zeros((2, zs, 128), jnp.float32).at[:, :, : extra.shape[0]].set(extra)
    chunks = jnp.concatenate([chunks, tail], axis=2)
    xl = lax.axis_index("xl")
    mine = lax.dynamic_index_in_dim(chunks, xl, 0, keepdims=False)
    other = lax.dynamic_index_in_dim(chunks, 1 - xl, 0, keepdims=False)
    pair_sum = mine + lax.ppermute(other, "xl", [(0, 1), (1, 0)])
    total = jnp.sum(lax.all_to_all(pair_sum, "z", 0, 0, tiled=True), axis=0)
    body = total[: sectors * share * cols].reshape((sectors, share, cols))
    return body, total[sectors * share * cols : sectors * share * cols + extra.shape[0]]


def gather_rows(rows_value, zs):
    sectors, share, cols = rows_value.shape
    spread = jnp.broadcast_to(rows_value[None], (zs,) + rows_value.shape)
    same = lax.all_to_all(spread, "z", 0, 0, tiled=True)
    other = lax.ppermute(same, "xl", [(0, 1), (1, 0)])
    xl = lax.axis_index("xl")
    pair = jnp.where(xl == 0, jnp.stack([same, other], 1), jnp.stack([other, same], 1))
    return pair.reshape((2 * zs, sectors, share, cols)).transpose(1, 0, 2, 3).reshape(
        (sectors, 2 * zs * share, cols)
    )


DEPTH = 3


def pair_kernel_dma(src_ref, side_ref, tgt_ref, cnt_ref, a_hbm, b_hbm, l_hbm, r_hbm, o_ref,
                    s_buf, l_buf, r_buf, sems):
    slots = l_hbm.shape[0]
    nbuf = s_buf.shape[0]
    count = jnp.clip(cnt_ref[0], 0, slots)

    def copies(k, slot):
        index = src_ref[k]
        from_a = pltpu.make_async_copy(a_hbm.at[index], s_buf.at[slot], sems.at[0, slot])
        from_b = pltpu.make_async_copy(b_hbm.at[index], s_buf.at[slot], sems.at[0, slot])
        left = pltpu.make_async_copy(l_hbm.at[k], l_buf.at[slot], sems.at[1, slot])
        right = pltpu.make_async_copy(r_hbm.at[k], r_buf.at[slot], sems.at[2, slot])
        return from_a, from_b, left, right

    def start(k):
        slot = k % nbuf
        from_a, from_b, left, right = copies(k, slot)

        @pl.when(side_ref[k] == 0)
        def _():
            from_a.start()

        @pl.when(side_ref[k] != 0)
        def _():
            from_b.start()

        left.start()
        right.start()

    o_ref[...] = jnp.zeros_like(o_ref)
    for k in range(DEPTH):
        @pl.when(k < count)
        def _():
            start(k)

    def body(k, carry):
        slot = k % nbuf
        pltpu.make_async_copy(a_hbm.at[0], s_buf.at[slot], sems.at[0, slot]).wait()
        pltpu.make_async_copy(l_hbm.at[0], l_buf.at[slot], sems.at[1, slot]).wait()
        pltpu.make_async_copy(r_hbm.at[0], r_buf.at[slot], sems.at[2, slot]).wait()

        @pl.when(k + DEPTH < count)
        def _():
            start(k + DEPTH)

        middle = jnp.dot(l_buf[slot], s_buf[slot], preferred_element_type=jnp.float32)
        high = middle.astype(jnp.bfloat16)
        low = (middle - high.astype(jnp.float32)).astype(jnp.bfloat16)
        rb = r_buf[slot]
        contribution = jnp.dot(high, rb, preferred_element_type=jnp.float32) + jnp.dot(
            low, rb, preferred_element_type=jnp.float32
        )
        t = tgt_ref[k]
        o_ref[t] = o_ref[t] + contribution
        return carry

    lax.fori_loop(0, count, body, 0)


def pair_call(src, side, tgt, cnt, a, b, l, r, sector_count):
    slots, bs, _ = l.shape
    nbuf = DEPTH + 1
    any_spec = pl.BlockSpec(memory_space=pl.ANY)
    smem = pl.BlockSpec(memory_space=pltpu.SMEM)
    return pl.pallas_call(
        pair_kernel_dma,
        in_specs=[smem, smem, smem, smem, any_spec, any_spec, any_spec, any_spec],
        out_specs=pl.BlockSpec(memory_space=pltpu.VMEM),
        out_shape=jax.ShapeDtypeStruct((sector_count, bs, bs), jnp.float32),
        scratch_shapes=[
            pltpu.VMEM((nbuf, bs, bs), jnp.bfloat16),
            pltpu.VMEM((nbuf, bs, bs), jnp.bfloat16),
            pltpu.VMEM((nbuf, bs, bs), jnp.bfloat16),
            pltpu.SemaphoreType.DMA((3, nbuf)),
        ],
    )(src, side, tgt, cnt, a, b, l, r)


def pair_partial(sources, left_blocks, right_blocks, source_index, target_index, live_count, sector_count):
    same_core, other_core = sources
    slots, block_size, _ = left_blocks.shape
    chips = same_core.shape[0]
    same_core = same_core.reshape((chips * sector_count, block_size, block_size))
    other_core = other_core.reshape((chips * sector_count, block_size, block_size))
    wanted = jnp.clip(source_index, 0, 2 * chips * sector_count - 1)
    side = (wanted >= chips * sector_count).astype(jnp.int32)
    within = wanted - side * chips * sector_count
    return pair_call(
        within, side, target_index, live_count, same_core, other_core, left_blocks, right_blocks, sector_count
    )


def on_device(
    wavefunction,
    diagonal,
    preconditioner,
    left_operator_blocks,
    right_operator_blocks,
    slot_source_sector,
    slot_target_sector,
    pair_count,
    left_dims,
    right_dims,
):
    sector_count = wavefunction.shape[0]
    block_size = wavefunction.shape[1]
    n_chip = lax.axis_size("chip")
    n_sec = n_chip * lax.axis_size("core")
    n_z = lax.axis_size("z")
    n_op = n_z * lax.axis_size("xl")
    share_rows = block_size // n_op
    sec_index = lax.axis_index(SEC)
    core_index = lax.axis_index("core")
    op_index = lax.axis_index(OP)
    first_sector = sec_index * sector_count
    row_start = op_index * share_rows
    entries = float(left_dims.shape[0] * block_size * block_size)
    own_mask = block_mask(
        lax.dynamic_slice_in_dim(left_dims, first_sector, sector_count),
        lax.dynamic_slice_in_dim(right_dims, first_sector, sector_count),
        block_size,
    )
    own_vector = jnp.where(own_mask, wavefunction, jnp.zeros_like(wavefunction))
    diag_view = diagonal.astype(jnp.float32)
    scale_view = preconditioner.astype(jnp.float32)
    vector_view = own_vector.astype(jnp.float32)

    owner = slot_source_sector // sector_count
    owner_core = owner % 2
    position = (owner_core != core_index).astype(jnp.int32) * n_chip + owner // 2
    source_index = position * sector_count + slot_source_sector % sector_count
    target_index = jnp.clip(slot_target_sector, 0, sector_count - 1)
    live_count = pair_count

    def apply_partial(field, weights):
        sources = gather_sec(field, n_chip)
        partial_value = pair_partial(
            sources,
            left_operator_blocks,
            right_operator_blocks,
            source_index,
            target_index,
            live_count,
            sector_count,
        )
        extra = jnp.stack([jnp.sum(w * partial_value) for w in weights] or [jnp.float32(0)])
        return reduce_scatter_rows(partial_value, extra, n_z)

    pair_rows, first_terms = apply_partial(own_vector, (vector_view,))
    norm_vector, correlation = reduce_vector(
        jnp.stack(
            [
                jnp.sum(vector_view * vector_view),
                jnp.sum(vector_view * diag_view * vector_view) + first_terms[0],
            ]
        ),
        SEC,
        n_sec,
    )
    pairs_first = gather_rows(pair_rows, n_z)
    sigma_first = jnp.where(own_mask, diag_view * vector_view + pairs_first, 0.0)
    rayleigh = correlation / norm_vector
    residual = sigma_first - rayleigh * vector_view
    scaled = scale_view * residual
    along_vector, scaled_square = reduce_vector(
        jnp.stack([jnp.sum(vector_view * scaled), jnp.sum(scaled * scaled)]), SEC, n_sec
    )
    orthogonal = scaled - along_vector / norm_vector * vector_view
    square_norm = scaled_square - along_vector * along_vector / norm_vector
    corr_view = (orthogonal * lax.rsqrt(square_norm / entries + 1e-06)).astype(jnp.bfloat16)

    corr_full = corr_view.astype(jnp.float32)
    pairs_second, pair_terms = apply_partial(corr_view, (vector_view, corr_full))
    mask_rows = lax.dynamic_slice_in_dim(own_mask, row_start, share_rows, 1)
    diag_rows = lax.dynamic_slice_in_dim(diag_view, row_start, share_rows, 1)
    corr_rows = lax.dynamic_slice_in_dim(corr_view, row_start, share_rows, 1).astype(jnp.float32)
    product_rows = jnp.where(mask_rows, diag_rows * corr_rows + pairs_second, 0.0)
    local_terms = jnp.stack(
        [jnp.sum(vector_view * diag_view * corr_full), jnp.sum(corr_full * diag_view * corr_full)]
    )
    cross_term, self_term = reduce_vector(local_terms + pair_terms, SEC, n_sec)
    projected = jnp.stack(
        [rayleigh, cross_term * lax.rsqrt(norm_vector * entries), self_term / entries]
    )
    return (corr_view, product_rows, projected)


def solution(mesh):
    n_sec, n_op = mesh.devices.shape
    mesh = Mesh(mesh.devices.reshape((n_sec // 2, 2, n_op // 2, 2)), ("chip", "core", "z", "xl"))
    in_specs = (
        P(SEC, None, None),
        P(SEC, None, None),
        P(SEC, None, None),
        P(("chip", "core", "z", "xl"), None, None),
        P(("chip", "core", "z", "xl"), None, None),
        P(("chip", "core", "z", "xl")),
        P(("chip", "core", "z", "xl")),
        P(("chip", "core", "z", "xl")),
        P(),
        P(),
    )
    out_specs = (P(SEC, None, None), P(SEC, OP, None), P())
    return jax.shard_map(
        on_device, mesh=mesh, in_specs=in_specs, out_specs=out_specs, check_vma=False
    )
```

```python
import functools

import jax
import jax.numpy as jnp
from jax import lax
from jax.experimental import pallas as pl
from jax.experimental.pallas import tpu as pltpu
from jax.sharding import Mesh, PartitionSpec as P


def block_mask(left_dims, right_dims, block_size):
    positions = jnp.arange(block_size, dtype=jnp.int32)
    return (positions[None, :, None] < left_dims[:, None, None]) & (
        positions[None, None, :] < right_dims[:, None, None]
    )


SEC = ("chip", "core")
OP = ("z", "xl")


def gather_sec(value, chips):
    spread = jnp.broadcast_to(value[None], (chips,) + value.shape)
    same_core = lax.all_to_all(spread, "chip", 0, 0, tiled=True)
    other_core = lax.ppermute(same_core, "core", [(0, 1), (1, 0)])
    return same_core, other_core


def ordered_gather(value, axis_name, count):
    spread = jnp.broadcast_to(value[None], (count,) + value.shape)
    return lax.all_to_all(spread, axis_name, 0, 0, tiled=True)


def reduce_vector(values, axis_name, count):
    return jnp.sum(ordered_gather(values, axis_name, count), axis=0)


def reduce_scatter_rows(partial_value, extra, zs):
    _, _, sectors, share, cols = partial_value.shape
    chunks = partial_value.reshape((2, zs, sectors * share * cols))
    tail = jnp.zeros((2, zs, 128), jnp.float32).at[:, :, : extra.shape[0]].set(extra)
    chunks = jnp.concatenate([chunks, tail], axis=2)
    xl = lax.axis_index("xl")
    mine = lax.dynamic_index_in_dim(chunks, xl, 0, keepdims=False)
    other = lax.dynamic_index_in_dim(chunks, 1 - xl, 0, keepdims=False)
    pair_sum = mine + lax.ppermute(other, "xl", [(0, 1), (1, 0)])
    total = jnp.sum(lax.all_to_all(pair_sum, "z", 0, 0, tiled=True), axis=0)
    body = total[: sectors * share * cols].reshape((sectors, share, cols))
    return body, total[sectors * share * cols : sectors * share * cols + extra.shape[0]]


def gather_rows(rows_value, zs):
    sectors, share, cols = rows_value.shape
    spread = jnp.broadcast_to(rows_value[None], (zs,) + rows_value.shape)
    same = lax.all_to_all(spread, "z", 0, 0, tiled=True)
    other = lax.ppermute(same, "xl", [(0, 1), (1, 0)])
    xl = lax.axis_index("xl")
    pair = jnp.where(xl == 0, jnp.stack([same, other], 1), jnp.stack([other, same], 1))
    return pair.reshape((2 * zs, sectors, share, cols)).transpose(1, 0, 2, 3).reshape(
        (sectors, 2 * zs * share, cols)
    )


DEPTH = 3


def pair_kernel_dma(src_ref, side_ref, tgt_ref, cnt_ref, a_hbm, b_hbm, l_hbm, r_hbm, o_ref,
                    s_buf, l_buf, r_buf, sems):
    slots = l_hbm.shape[0]
    nbuf = s_buf.shape[0]
    count = jnp.clip(cnt_ref[0], 0, slots)

    def copies(k, slot):
        index = src_ref[k]
        from_a = pltpu.make_async_copy(a_hbm.at[index], s_buf.at[slot], sems.at[0, slot])
        from_b = pltpu.make_async_copy(b_hbm.at[index], s_buf.at[slot], sems.at[0, slot])
        left = pltpu.make_async_copy(l_hbm.at[k], l_buf.at[slot], sems.at[1, slot])
        right = pltpu.make_async_copy(r_hbm.at[k], r_buf.at[slot], sems.at[2, slot])
        return from_a, from_b, left, right

    def start(k):
        slot = k % nbuf
        from_a, from_b, left, right = copies(k, slot)

        @pl.when(side_ref[k] == 0)
        def _():
            from_a.start()

        @pl.when(side_ref[k] != 0)
        def _():
            from_b.start()

        left.start()
        right.start()

    o_ref[...] = jnp.zeros_like(o_ref)
    for k in range(DEPTH):
        @pl.when(k < count)
        def _():
            start(k)

    def body(k, carry):
        slot = k % nbuf
        pltpu.make_async_copy(a_hbm.at[0], s_buf.at[slot], sems.at[0, slot]).wait()
        pltpu.make_async_copy(l_hbm.at[0], l_buf.at[slot], sems.at[1, slot]).wait()
        pltpu.make_async_copy(r_hbm.at[0], r_buf.at[slot], sems.at[2, slot]).wait()

        @pl.when(k + DEPTH < count)
        def _():
            start(k + DEPTH)

        middle = jnp.dot(l_buf[slot], s_buf[slot], preferred_element_type=jnp.float32)
        high = middle.astype(jnp.bfloat16)
        low = (middle - high.astype(jnp.float32)).astype(jnp.bfloat16)
        rb = r_buf[slot]
        contribution = jnp.dot(high, rb, preferred_element_type=jnp.float32) + jnp.dot(
            low, rb, preferred_element_type=jnp.float32
        )
        t = tgt_ref[k]
        lanes = o_ref.shape[0]
        pieces = contribution.reshape((o_ref.shape[1], lanes) + o_ref.shape[3:])
        for x in range(lanes):
            o_ref[x, :, t] = o_ref[x, :, t] + pieces[:, x]
        return carry

    lax.fori_loop(0, count, body, 0)


def pair_call(src, side, tgt, cnt, a, b, l, r, sector_count, zs):
    slots, bs, _ = l.shape
    nbuf = DEPTH + 1
    any_spec = pl.BlockSpec(memory_space=pl.ANY)
    smem = pl.BlockSpec(memory_space=pltpu.SMEM)
    return pl.pallas_call(
        pair_kernel_dma,
        in_specs=[smem, smem, smem, smem, any_spec, any_spec, any_spec, any_spec],
        out_specs=pl.BlockSpec(memory_space=pltpu.VMEM),
        out_shape=jax.ShapeDtypeStruct((2, zs, sector_count, bs // (2 * zs), bs), jnp.float32),
        scratch_shapes=[
            pltpu.VMEM((nbuf, bs, bs), jnp.bfloat16),
            pltpu.VMEM((nbuf, bs, bs), jnp.bfloat16),
            pltpu.VMEM((nbuf, bs, bs), jnp.bfloat16),
            pltpu.SemaphoreType.DMA((3, nbuf)),
        ],
    )(src, side, tgt, cnt, a, b, l, r)


def pair_partial(sources, left_blocks, right_blocks, source_index, target_index, live_count, sector_count, zs):
    same_core, other_core = sources
    slots, block_size, _ = left_blocks.shape
    chips = same_core.shape[0]
    same_core = same_core.reshape((chips * sector_count, block_size, block_size))
    other_core = other_core.reshape((chips * sector_count, block_size, block_size))
    wanted = jnp.clip(source_index, 0, 2 * chips * sector_count - 1)
    side = (wanted >= chips * sector_count).astype(jnp.int32)
    within = wanted - side * chips * sector_count
    return pair_call(
        within, side, target_index, live_count, same_core, other_core, left_blocks, right_blocks,
        sector_count, zs,
    )


def on_device(
    wavefunction,
    diagonal,
    preconditioner,
    left_operator_blocks,
    right_operator_blocks,
    slot_source_sector,
    slot_target_sector,
    pair_count,
    left_dims,
    right_dims,
):
    sector_count = wavefunction.shape[0]
    block_size = wavefunction.shape[1]
    n_chip = lax.axis_size("chip")
    n_sec = n_chip * lax.axis_size("core")
    n_z = lax.axis_size("z")
    n_op = n_z * lax.axis_size("xl")
    share_rows = block_size // n_op
    sec_index = lax.axis_index(SEC)
    core_index = lax.axis_index("core")
    op_index = lax.axis_index(OP)
    first_sector = sec_index * sector_count
    row_start = op_index * share_rows
    entries = float(left_dims.shape[0] * block_size * block_size)
    own_mask = block_mask(
        lax.dynamic_slice_in_dim(left_dims, first_sector, sector_count),
        lax.dynamic_slice_in_dim(right_dims, first_sector, sector_count),
        block_size,
    )
    own_vector = jnp.where(own_mask, wavefunction, jnp.zeros_like(wavefunction))
    diag_view = diagonal.astype(jnp.float32)
    scale_view = preconditioner.astype(jnp.float32)
    vector_view = own_vector.astype(jnp.float32)

    owner = slot_source_sector // sector_count
    owner_core = owner % 2
    position = (owner_core != core_index).astype(jnp.int32) * n_chip + owner // 2
    source_index = position * sector_count + slot_source_sector % sector_count
    target_index = jnp.clip(slot_target_sector, 0, sector_count - 1)
    live_count = pair_count

    def apply_partial(field, weights):
        sources = gather_sec(field, n_chip)
        partial_value = pair_partial(
            sources,
            left_operator_blocks,
            right_operator_blocks,
            source_index,
            target_index,
            live_count,
            sector_count,
            n_z,
        )

        def laid_out(w):
            return w.reshape((sector_count, n_z, 2, share_rows, block_size)).transpose(2, 1, 0, 3, 4)

        extra = jnp.stack(
            [jnp.sum(laid_out(w) * partial_value) for w in weights] or [jnp.float32(0)]
        )
        return reduce_scatter_rows(partial_value, extra, n_z)

    pair_rows, first_terms = apply_partial(own_vector, (vector_view,))
    norm_vector, correlation = reduce_vector(
        jnp.stack(
            [
                jnp.sum(vector_view * vector_view),
                jnp.sum(vector_view * diag_view * vector_view) + first_terms[0],
            ]
        ),
        SEC,
        n_sec,
    )
    pairs_first = gather_rows(pair_rows, n_z)
    sigma_first = jnp.where(own_mask, diag_view * vector_view + pairs_first, 0.0)
    rayleigh = correlation / norm_vector
    residual = sigma_first - rayleigh * vector_view
    scaled = scale_view * residual
    along_vector, scaled_square = reduce_vector(
        jnp.stack([jnp.sum(vector_view * scaled), jnp.sum(scaled * scaled)]), SEC, n_sec
    )
    orthogonal = scaled - along_vector / norm_vector * vector_view
    square_norm = scaled_square - along_vector * along_vector / norm_vector
    corr_view = (orthogonal * lax.rsqrt(square_norm / entries + 1e-06)).astype(jnp.bfloat16)

    corr_full = corr_view.astype(jnp.float32)
    pairs_second, pair_terms = apply_partial(corr_view, (vector_view, corr_full))
    mask_rows = lax.dynamic_slice_in_dim(own_mask, row_start, share_rows, 1)
    diag_rows = lax.dynamic_slice_in_dim(diag_view, row_start, share_rows, 1)
    corr_rows = lax.dynamic_slice_in_dim(corr_view, row_start, share_rows, 1).astype(jnp.float32)
    product_rows = jnp.where(mask_rows, diag_rows * corr_rows + pairs_second, 0.0)
    local_terms = jnp.stack(
        [jnp.sum(vector_view * diag_view * corr_full), jnp.sum(corr_full * diag_view * corr_full)]
    )
    cross_term, self_term = reduce_vector(local_terms + pair_terms, SEC, n_sec)
    projected = jnp.stack(
        [rayleigh, cross_term * lax.rsqrt(norm_vector * entries), self_term / entries]
    )
    return (corr_view, product_rows, projected)


def solution(mesh):
    n_sec, n_op = mesh.devices.shape
    mesh = Mesh(mesh.devices.reshape((n_sec // 2, 2, n_op // 2, 2)), ("chip", "core", "z", "xl"))
    in_specs = (
        P(SEC, None, None),
        P(SEC, None, None),
        P(SEC, None, None),
        P(("chip", "core", "z", "xl"), None, None),
        P(("chip", "core", "z", "xl"), None, None),
        P(("chip", "core", "z", "xl")),
        P(("chip", "core", "z", "xl")),
        P(("chip", "core", "z", "xl")),
        P(),
        P(),
    )
    out_specs = (P(SEC, None, None), P(SEC, OP, None), P())
    return jax.shard_map(
        on_device, mesh=mesh, in_specs=in_specs, out_specs=out_specs, check_vma=False
    )
```

```python
import functools

import jax
import jax.numpy as jnp
from jax import lax
from jax.experimental import pallas as pl
from jax.experimental.pallas import tpu as pltpu
from jax.sharding import Mesh, PartitionSpec as P


def block_mask(left_dims, right_dims, block_size):
    positions = jnp.arange(block_size, dtype=jnp.int32)
    return (positions[None, :, None] < left_dims[:, None, None]) & (
        positions[None, None, :] < right_dims[:, None, None]
    )


SEC = ("chip", "core")
OP = ("z", "xl")


def gather_sec(value, chips):
    spread = jnp.broadcast_to(value[None], (chips,) + value.shape)
    same_core = lax.all_to_all(spread, "chip", 0, 0, tiled=True)
    other_core = lax.ppermute(same_core, "core", [(0, 1), (1, 0)])
    return same_core, other_core


def ordered_gather(value, axis_name, count):
    spread = jnp.broadcast_to(value[None], (count,) + value.shape)
    return lax.all_to_all(spread, axis_name, 0, 0, tiled=True)


def reduce_vector(values, axis_name, count):
    return jnp.sum(ordered_gather(values, axis_name, count), axis=0)


def reduce_scatter_rows(partial_value, extra, zs):
    sectors, rows, cols = partial_value.shape
    share = rows // (2 * zs)
    chunks = partial_value.reshape((sectors, zs, 2, share, cols)).transpose(2, 1, 0, 3, 4)
    chunks = chunks.reshape((2, zs, sectors * share * cols))
    tail = jnp.zeros((2, zs, 128), jnp.float32).at[:, :, : extra.shape[0]].set(extra)
    chunks = jnp.concatenate([chunks, tail], axis=2)
    xl = lax.axis_index("xl")
    mine = lax.dynamic_index_in_dim(chunks, xl, 0, keepdims=False)
    other = lax.dynamic_index_in_dim(chunks, 1 - xl, 0, keepdims=False)
    pair_sum = mine + lax.ppermute(other, "xl", [(0, 1), (1, 0)])
    total = jnp.sum(lax.all_to_all(pair_sum, "z", 0, 0, tiled=True), axis=0)
    body = total[: sectors * share * cols].reshape((sectors, share, cols))
    return body, total[sectors * share * cols : sectors * share * cols + extra.shape[0]]


def gather_rows(rows_value, zs):
    sectors, share, cols = rows_value.shape
    xl = lax.axis_index("xl")
    other = lax.ppermute(rows_value, "xl", [(0, 1), (1, 0)])
    pair = jnp.where(xl == 0, jnp.stack([rows_value, other]), jnp.stack([other, rows_value]))
    spread = jnp.broadcast_to(pair[None], (zs,) + pair.shape)
    every = lax.all_to_all(spread, "z", 0, 0, tiled=True)
    return every.reshape((2 * zs, sectors, share, cols)).transpose(1, 0, 2, 3).reshape(
        (sectors, 2 * zs * share, cols)
    )


DEPTH = 3


def pair_kernel_dma(src_ref, side_ref, tgt_ref, cnt_ref, a_hbm, b_hbm, l_hbm, r_hbm, o_ref,
                    s_buf, l_buf, r_buf, sems):
    slots = l_hbm.shape[0]
    nbuf = s_buf.shape[0]
    count = jnp.clip(cnt_ref[0], 0, slots)

    def copies(k, slot):
        index = src_ref[k]
        from_a = pltpu.make_async_copy(a_hbm.at[index], s_buf.at[slot], sems.at[0, slot])
        from_b = pltpu.make_async_copy(b_hbm.at[index], s_buf.at[slot], sems.at[0, slot])
        left = pltpu.make_async_copy(l_hbm.at[k], l_buf.at[slot], sems.at[1, slot])
        right = pltpu.make_async_copy(r_hbm.at[k], r_buf.at[slot], sems.at[2, slot])
        return from_a, from_b, left, right

    def start(k):
        slot = k % nbuf
        from_a, from_b, left, right = copies(k, slot)

        @pl.when(side_ref[k] == 0)
        def _():
            from_a.start()

        @pl.when(side_ref[k] != 0)
        def _():
            from_b.start()

        left.start()
        right.start()

    o_ref[...] = jnp.zeros_like(o_ref)
    for k in range(DEPTH):
        @pl.when(k < count)
        def _():
            start(k)

    def body(k, carry):
        slot = k % nbuf
        pltpu.make_async_copy(a_hbm.at[0], s_buf.at[slot], sems.at[0, slot]).wait()
        pltpu.make_async_copy(l_hbm.at[0], l_buf.at[slot], sems.at[1, slot]).wait()
        pltpu.make_async_copy(r_hbm.at[0], r_buf.at[slot], sems.at[2, slot]).wait()

        @pl.when(k + DEPTH < count)
        def _():
            start(k + DEPTH)

        middle = jnp.dot(l_buf[slot], s_buf[slot], preferred_element_type=jnp.float32)
        high = middle.astype(jnp.bfloat16)
        low = (middle - high.astype(jnp.float32)).astype(jnp.bfloat16)
        rb = r_buf[slot]
        contribution = jnp.dot(high, rb, preferred_element_type=jnp.float32) + jnp.dot(
            low, rb, preferred_element_type=jnp.float32
        )
        t = tgt_ref[k]
        o_ref[t] = o_ref[t] + contribution
        return carry

    lax.fori_loop(0, count, body, 0)


def pair_call(src, side, tgt, cnt, a, b, l, r, sector_count):
    slots, bs, _ = l.shape
    nbuf = DEPTH + 1
    any_spec = pl.BlockSpec(memory_space=pl.ANY)
    smem = pl.BlockSpec(memory_space=pltpu.SMEM)
    return pl.pallas_call(
        pair_kernel_dma,
        in_specs=[smem, smem, smem, smem, any_spec, any_spec, any_spec, any_spec],
        out_specs=pl.BlockSpec(memory_space=pltpu.VMEM),
        out_shape=jax.ShapeDtypeStruct((sector_count, bs, bs), jnp.float32),
        scratch_shapes=[
            pltpu.VMEM((nbuf, bs, bs), jnp.bfloat16),
            pltpu.VMEM((nbuf, bs, bs), jnp.bfloat16),
            pltpu.VMEM((nbuf, bs, bs), jnp.bfloat16),
            pltpu.SemaphoreType.DMA((3, nbuf)),
        ],
    )(src, side, tgt, cnt, a, b, l, r)


def pair_partial(sources, left_blocks, right_blocks, source_index, target_index, live_count, sector_count):
    same_core, other_core = sources
    slots, block_size, _ = left_blocks.shape
    chips = same_core.shape[0]
    same_core = same_core.reshape((chips * sector_count, block_size, block_size))
    other_core = other_core.reshape((chips * sector_count, block_size, block_size))
    wanted = jnp.clip(source_index, 0, 2 * chips * sector_count - 1)
    side = (wanted >= chips * sector_count).astype(jnp.int32)
    within = wanted - side * chips * sector_count
    return pair_call(
        within, side, target_index, live_count, same_core, other_core, left_blocks, right_blocks, sector_count
    )


def on_device(
    wavefunction,
    diagonal,
    preconditioner,
    left_operator_blocks,
    right_operator_blocks,
    slot_source_sector,
    slot_target_sector,
    pair_count,
    left_dims,
    right_dims,
):
    sector_count = wavefunction.shape[0]
    block_size = wavefunction.shape[1]
    n_chip = lax.axis_size("chip")
    n_sec = n_chip * lax.axis_size("core")
    n_z = lax.axis_size("z")
    n_op = n_z * lax.axis_size("xl")
    share_rows = block_size // n_op
    sec_index = lax.axis_index(SEC)
    core_index = lax.axis_index("core")
    op_index = lax.axis_index(OP)
    first_sector = sec_index * sector_count
    row_start = op_index * share_rows
    entries = float(left_dims.shape[0] * block_size * block_size)
    own_mask = block_mask(
        lax.dynamic_slice_in_dim(left_dims, first_sector, sector_count),
        lax.dynamic_slice_in_dim(right_dims, first_sector, sector_count),
        block_size,
    )
    own_vector = jnp.where(own_mask, wavefunction, jnp.zeros_like(wavefunction))
    diag_view = diagonal.astype(jnp.float32)
    scale_view = preconditioner.astype(jnp.float32)
    vector_view = own_vector.astype(jnp.float32)

    owner = slot_source_sector // sector_count
    owner_core = owner % 2
    position = (owner_core != core_index).astype(jnp.int32) * n_chip + owner // 2
    source_index = position * sector_count + slot_source_sector % sector_count
    target_index = jnp.clip(slot_target_sector, 0, sector_count - 1)
    live_count = pair_count

    def apply_partial(field, weights):
        sources = gather_sec(field, n_chip)
        partial_value = pair_partial(
            sources,
            left_operator_blocks,
            right_operator_blocks,
            source_index,
            target_index,
            live_count,
            sector_count,
        )
        extra = jnp.stack([jnp.sum(w * partial_value) for w in weights] or [jnp.float32(0)])
        return reduce_scatter_rows(partial_value, extra, n_z)

    pair_rows, first_terms = apply_partial(own_vector, (vector_view,))
    norm_vector, correlation = reduce_vector(
        jnp.stack(
            [
                jnp.sum(vector_view * vector_view),
                jnp.sum(vector_view * diag_view * vector_view) + first_terms[0],
            ]
        ),
        SEC,
        n_sec,
    )
    pairs_first = gather_rows(pair_rows, n_z)
    sigma_first = jnp.where(own_mask, diag_view * vector_view + pairs_first, 0.0)
    rayleigh = correlation / norm_vector
    residual = sigma_first - rayleigh * vector_view
    scaled = scale_view * residual
    along_vector, scaled_square = reduce_vector(
        jnp.stack([jnp.sum(vector_view * scaled), jnp.sum(scaled * scaled)]), SEC, n_sec
    )
    orthogonal = scaled - along_vector / norm_vector * vector_view
    square_norm = scaled_square - along_vector * along_vector / norm_vector
    corr_view = (orthogonal * lax.rsqrt(square_norm / entries + 1e-06)).astype(jnp.bfloat16)

    corr_full = corr_view.astype(jnp.float32)
    pairs_second, pair_terms = apply_partial(corr_view, (vector_view, corr_full))
    mask_rows = lax.dynamic_slice_in_dim(own_mask, row_start, share_rows, 1)
    diag_rows = lax.dynamic_slice_in_dim(diag_view, row_start, share_rows, 1)
    corr_rows = lax.dynamic_slice_in_dim(corr_view, row_start, share_rows, 1).astype(jnp.float32)
    product_rows = jnp.where(mask_rows, diag_rows * corr_rows + pairs_second, 0.0)
    local_terms = jnp.stack(
        [jnp.sum(vector_view * diag_view * corr_full), jnp.sum(corr_full * diag_view * corr_full)]
    )
    cross_term, self_term = reduce_vector(local_terms + pair_terms, SEC, n_sec)
    projected = jnp.stack(
        [rayleigh, cross_term * lax.rsqrt(norm_vector * entries), self_term / entries]
    )
    return (corr_view, product_rows, projected)


def solution(mesh):
    n_sec, n_op = mesh.devices.shape
    mesh = Mesh(mesh.devices.reshape((n_sec // 2, 2, n_op // 2, 2)), ("chip", "core", "z", "xl"))
    in_specs = (
        P(SEC, None, None),
        P(SEC, None, None),
        P(SEC, None, None),
        P(("chip", "core", "z", "xl"), None, None),
        P(("chip", "core", "z", "xl"), None, None),
        P(("chip", "core", "z", "xl")),
        P(("chip", "core", "z", "xl")),
        P(("chip", "core", "z", "xl")),
        P(),
        P(),
    )
    out_specs = (P(SEC, None, None), P(SEC, OP, None), P())
    return jax.shard_map(
        on_device, mesh=mesh, in_specs=in_specs, out_specs=out_specs, check_vma=False
    )
```

```python
import functools

import jax
import jax.numpy as jnp
from jax import lax
from jax.experimental import pallas as pl
from jax.experimental.pallas import tpu as pltpu
from jax.sharding import Mesh, PartitionSpec as P


def block_mask(left_dims, right_dims, block_size):
    positions = jnp.arange(block_size, dtype=jnp.int32)
    return (positions[None, :, None] < left_dims[:, None, None]) & (
        positions[None, None, :] < right_dims[:, None, None]
    )


SEC = ("chip", "core")
OP = ("z", "xl")


def gather_sec(value, chips):
    spread = jnp.broadcast_to(value[None], (chips,) + value.shape)
    same_core = lax.all_to_all(spread, "chip", 0, 0, tiled=True)
    other_core = lax.ppermute(same_core, "core", [(0, 1), (1, 0)])
    return same_core, other_core


def ordered_gather(value, axis_name, count):
    spread = jnp.broadcast_to(value[None], (count,) + value.shape)
    return lax.all_to_all(spread, axis_name, 0, 0, tiled=True)


def reduce_vector(values, axis_name, count):
    return jnp.sum(ordered_gather(values, axis_name, count), axis=0)


def reduce_scatter_rows(partial_value, extra, zs):
    sectors, rows, cols = partial_value.shape
    share = rows // (2 * zs)
    chunks = partial_value.reshape((sectors, zs, 2, share, cols)).transpose(2, 1, 0, 3, 4)
    chunks = chunks.reshape((2, zs, sectors * share * cols))
    tail = jnp.zeros((2, zs, 128), jnp.float32).at[:, :, : extra.shape[0]].set(extra)
    chunks = jnp.concatenate([chunks, tail], axis=2)
    xl = lax.axis_index("xl")
    mine = lax.dynamic_index_in_dim(chunks, xl, 0, keepdims=False)
    other = lax.dynamic_index_in_dim(chunks, 1 - xl, 0, keepdims=False)
    pair_sum = mine + lax.ppermute(other, "xl", [(0, 1), (1, 0)])
    total = jnp.sum(lax.all_to_all(pair_sum, "z", 0, 0, tiled=True), axis=0)
    body = total[: sectors * share * cols].reshape((sectors, share, cols))
    return body, total[sectors * share * cols : sectors * share * cols + extra.shape[0]]


def gather_rows(rows_value, zs):
    sectors, share, cols = rows_value.shape
    spread = jnp.broadcast_to(rows_value[None], (zs,) + rows_value.shape)
    same = lax.all_to_all(spread, "z", 0, 0, tiled=True)
    other = lax.ppermute(same, "xl", [(0, 1), (1, 0)])
    xl = lax.axis_index("xl")
    pair = jnp.where(xl == 0, jnp.stack([same, other], 1), jnp.stack([other, same], 1))
    return pair.reshape((2 * zs, sectors, share, cols)).transpose(1, 0, 2, 3).reshape(
        (sectors, 2 * zs * share, cols)
    )


DEPTH = 4


def pair_kernel_dma(src_ref, side_ref, tgt_ref, cnt_ref, a_hbm, b_hbm, l_hbm, r_hbm, o_ref,
                    s_buf, l_buf, r_buf, sems):
    slots = l_hbm.shape[0]
    nbuf = s_buf.shape[0]
    count = jnp.clip(cnt_ref[0], 0, slots)

    def copies(k, slot):
        index = src_ref[k]
        from_a = pltpu.make_async_copy(a_hbm.at[index], s_buf.at[slot], sems.at[0, slot])
        from_b = pltpu.make_async_copy(b_hbm.at[index], s_buf.at[slot], sems.at[0, slot])
        left = pltpu.make_async_copy(l_hbm.at[k], l_buf.at[slot], sems.at[1, slot])
        right = pltpu.make_async_copy(r_hbm.at[k], r_buf.at[slot], sems.at[2, slot])
        return from_a, from_b, left, right

    def start(k):
        slot = k % nbuf
        from_a, from_b, left, right = copies(k, slot)

        @pl.when(side_ref[k] == 0)
        def _():
            from_a.start()

        @pl.when(side_ref[k] != 0)
        def _():
            from_b.start()

        left.start()
        right.start()

    o_ref[...] = jnp.zeros_like(o_ref)
    for k in range(DEPTH):
        @pl.when(k < count)
        def _():
            start(k)

    def body(k, carry):
        slot = k % nbuf
        pltpu.make_async_copy(a_hbm.at[0], s_buf.at[slot], sems.at[0, slot]).wait()
        pltpu.make_async_copy(l_hbm.at[0], l_buf.at[slot], sems.at[1, slot]).wait()
        pltpu.make_async_copy(r_hbm.at[0], r_buf.at[slot], sems.at[2, slot]).wait()

        @pl.when(k + DEPTH < count)
        def _():
            start(k + DEPTH)

        middle = jnp.dot(l_buf[slot], s_buf[slot], preferred_element_type=jnp.float32)
        high = middle.astype(jnp.bfloat16)
        low = (middle - high.astype(jnp.float32)).astype(jnp.bfloat16)
        rb = r_buf[slot]
        contribution = jnp.dot(high, rb, preferred_element_type=jnp.float32) + jnp.dot(
            low, rb, preferred_element_type=jnp.float32
        )
        t = tgt_ref[k]
        o_ref[t] = o_ref[t] + contribution
        return carry

    lax.fori_loop(0, count, body, 0)


def pair_call(src, side, tgt, cnt, a, b, l, r, sector_count):
    slots, bs, _ = l.shape
    nbuf = DEPTH + 1
    any_spec = pl.BlockSpec(memory_space=pl.ANY)
    smem = pl.BlockSpec(memory_space=pltpu.SMEM)
    return pl.pallas_call(
        pair_kernel_dma,
        in_specs=[smem, smem, smem, smem, any_spec, any_spec, any_spec, any_spec],
        out_specs=pl.BlockSpec(memory_space=pltpu.VMEM),
        out_shape=jax.ShapeDtypeStruct((sector_count, bs, bs), jnp.float32),
        scratch_shapes=[
            pltpu.VMEM((nbuf, bs, bs), jnp.bfloat16),
            pltpu.VMEM((nbuf, bs, bs), jnp.bfloat16),
            pltpu.VMEM((nbuf, bs, bs), jnp.bfloat16),
            pltpu.SemaphoreType.DMA((3, nbuf)),
        ],
    )(src, side, tgt, cnt, a, b, l, r)


def pair_partial(sources, left_blocks, right_blocks, source_index, target_index, live_count, sector_count):
    same_core, other_core = sources
    slots, block_size, _ = left_blocks.shape
    chips = same_core.shape[0]
    same_core = same_core.reshape((chips * sector_count, block_size, block_size))
    other_core = other_core.reshape((chips * sector_count, block_size, block_size))
    wanted = jnp.clip(source_index, 0, 2 * chips * sector_count - 1)
    side = (wanted >= chips * sector_count).astype(jnp.int32)
    within = wanted - side * chips * sector_count
    return pair_call(
        within, side, target_index, live_count, same_core, other_core, left_blocks, right_blocks, sector_count
    )


def on_device(
    wavefunction,
    diagonal,
    preconditioner,
    left_operator_blocks,
    right_operator_blocks,
    slot_source_sector,
    slot_target_sector,
    pair_count,
    left_dims,
    right_dims,
):
    sector_count = wavefunction.shape[0]
    block_size = wavefunction.shape[1]
    n_chip = lax.axis_size("chip")
    n_sec = n_chip * lax.axis_size("core")
    n_z = lax.axis_size("z")
    n_op = n_z * lax.axis_size("xl")
    share_rows = block_size // n_op
    sec_index = lax.axis_index(SEC)
    core_index = lax.axis_index("core")
    op_index = lax.axis_index(OP)
    first_sector = sec_index * sector_count
    row_start = op_index * share_rows
    entries = float(left_dims.shape[0] * block_size * block_size)
    own_mask = block_mask(
        lax.dynamic_slice_in_dim(left_dims, first_sector, sector_count),
        lax.dynamic_slice_in_dim(right_dims, first_sector, sector_count),
        block_size,
    )
    own_vector = jnp.where(own_mask, wavefunction, jnp.zeros_like(wavefunction))
    diag_view = diagonal.astype(jnp.float32)
    scale_view = preconditioner.astype(jnp.float32)
    vector_view = own_vector.astype(jnp.float32)

    owner = slot_source_sector // sector_count
    owner_core = owner % 2
    position = (owner_core != core_index).astype(jnp.int32) * n_chip + owner // 2
    source_index = position * sector_count + slot_source_sector % sector_count
    target_index = jnp.clip(slot_target_sector, 0, sector_count - 1)
    live_count = pair_count

    def apply_partial(field, weights):
        sources = gather_sec(field, n_chip)
        partial_value = pair_partial(
            sources,
            left_operator_blocks,
            right_operator_blocks,
            source_index,
            target_index,
            live_count,
            sector_count,
        )
        extra = jnp.stack([jnp.sum(w * partial_value) for w in weights] or [jnp.float32(0)])
        return reduce_scatter_rows(partial_value, extra, n_z)

    pair_rows, first_terms = apply_partial(own_vector, (vector_view,))
    norm_vector, correlation = reduce_vector(
        jnp.stack(
            [
                jnp.sum(vector_view * vector_view),
                jnp.sum(vector_view * diag_view * vector_view) + first_terms[0],
            ]
        ),
        SEC,
        n_sec,
    )
    pairs_first = gather_rows(pair_rows, n_z)
    sigma_first = jnp.where(own_mask, diag_view * vector_view + pairs_first, 0.0)
    rayleigh = correlation / norm_vector
    residual = sigma_first - rayleigh * vector_view
    scaled = scale_view * residual
    along_vector, scaled_square = reduce_vector(
        jnp.stack([jnp.sum(vector_view * scaled), jnp.sum(scaled * scaled)]), SEC, n_sec
    )
    orthogonal = scaled - along_vector / norm_vector * vector_view
    square_norm = scaled_square - along_vector * along_vector / norm_vector
    corr_view = (orthogonal * lax.rsqrt(square_norm / entries + 1e-06)).astype(jnp.bfloat16)

    corr_full = corr_view.astype(jnp.float32)
    pairs_second, pair_terms = apply_partial(corr_view, (vector_view, corr_full))
    mask_rows = lax.dynamic_slice_in_dim(own_mask, row_start, share_rows, 1)
    diag_rows = lax.dynamic_slice_in_dim(diag_view, row_start, share_rows, 1)
    corr_rows = lax.dynamic_slice_in_dim(corr_view, row_start, share_rows, 1).astype(jnp.float32)
    product_rows = jnp.where(mask_rows, diag_rows * corr_rows + pairs_second, 0.0)
    local_terms = jnp.stack(
        [jnp.sum(vector_view * diag_view * corr_full), jnp.sum(corr_full * diag_view * corr_full)]
    )
    cross_term, self_term = reduce_vector(local_terms + pair_terms, SEC, n_sec)
    projected = jnp.stack(
        [rayleigh, cross_term * lax.rsqrt(norm_vector * entries), self_term / entries]
    )
    return (corr_view, product_rows, projected)


def solution(mesh):
    n_sec, n_op = mesh.devices.shape
    mesh = Mesh(mesh.devices.reshape((n_sec // 2, 2, n_op // 2, 2)), ("chip", "core", "z", "xl"))
    in_specs = (
        P(SEC, None, None),
        P(SEC, None, None),
        P(SEC, None, None),
        P(("chip", "core", "z", "xl"), None, None),
        P(("chip", "core", "z", "xl"), None, None),
        P(("chip", "core", "z", "xl")),
        P(("chip", "core", "z", "xl")),
        P(("chip", "core", "z", "xl")),
        P(),
        P(),
    )
    out_specs = (P(SEC, None, None), P(SEC, OP, None), P())
    return jax.shard_map(
        on_device, mesh=mesh, in_specs=in_specs, out_specs=out_specs, check_vma=False
    )
```
